128 devices in a mesh: blk: 32 (over z, y, core), gz: 4 (over x).
Axes of the slice: x: 4, y: 4, z: 4, core: 2. Of those that a mesh axis runs over, the one named last changes fastest.
Arguments:
- adjoint: float32 [4, 256, 19, 16, 256], P('gz', 'blk'), may hold values from -6 to 6
- velocity: float32 [4, 256, 3, 16, 256], P('gz', 'blk'), may hold values from -0.32 to 0.32
- porosity: float32 [4, 256, 16, 256], P('gz', 'blk'), may hold values from 0 to 1
- block_x: int32 [4, 256], P('gz'), may hold values from 0 to 31, as said below
- neighbours: int32 [4, 256, 6], P('gz'), may hold values from -1 to 255, as said below
- owner_map: int32 [32], replicated, may hold values from 1 to 6, 64 in all
Outputs:
- adjoint_out: float32 [4, 256, 19, 16, 256], P('gz', 'blk')
- smoothed: float32 [4, 32, 12, 16, 512], P('gz', 'blk')
The draws below stay inside these ranges and needn't reach their ends.
Inputs may be any that keep to these rules, and one draw needn't show every extreme that they name: `block_x`: in every layer, block row k holds 32 blocks, one on each device of blk at that device's slot k (slot = device * 8 + k); the columns of one row of one layer are all different. `neighbours`: the entries name the blocks beside a slot in the same row (-x, +x), in the rows k - 1 and k + 1 (-y, +y) and at the same row and column in the layer below and above (-z, +z), as slots of that layer; -1 beyond the window's faces. Design slab j of every layer holds the 2 * owner_map[j] cell rows after those of slabs 0 to j - 1; the entries sum to 64.
All inputs are finite; a program needn't handle non-finite values.
Results may differ from the reference program's by a relative error of at most 0.0001.
Values sent between devices are 32-bit elements; how exact they have to be, the bound alone decides.
A program may use at most 128 MiB of HBM per device.

```python
import math
import jax
import jax.numpy as jnp
import numpy as np
from jax import lax

B = 16
K = 8
STEPS = 2
LAYERS = 4
COLS = 32
SLOTS = 256
UNITS = 64
MOSTU = 6
ROWS = 12


def layout_columns(key):
    base = jax.random.fold_in(key, 7)
    keys_all = jax.random.split(base, LAYERS * K)
    orders = jax.vmap(lambda single: jax.random.permutation(single, COLS))(keys_all)
    return orders.reshape(LAYERS, K, COLS).astype(jnp.int32)


def draw_block_x(key, part):
    orders = layout_columns(key)
    inverse = jnp.argsort(orders, axis=-1).astype(jnp.int32)
    return jnp.transpose(inverse, (0, 2, 1)).reshape(LAYERS, SLOTS)


def draw_neighbours(key, part):
    orders = layout_columns(key)
    row_ids = jnp.arange(K, dtype=jnp.int32)[None, :, None]
    slot_grid = orders * K + row_ids
    empty_col = jnp.full((LAYERS, K, 1), -1, jnp.int32)
    empty_row = jnp.full((LAYERS, 1, COLS), -1, jnp.int32)
    empty_layer = jnp.full((1, K, COLS), -1, jnp.int32)
    minus_x = jnp.concatenate([empty_col, slot_grid[:, :, :-1]], axis=2)
    plus_x = jnp.concatenate([slot_grid[:, :, 1:], empty_col], axis=2)
    minus_y = jnp.concatenate([empty_row, slot_grid[:, :-1, :]], axis=1)
    plus_y = jnp.concatenate([slot_grid[:, 1:, :], empty_row], axis=1)
    minus_z = jnp.concatenate([empty_layer, slot_grid[:-1]], axis=0)
    plus_z = jnp.concatenate([slot_grid[1:], empty_layer], axis=0)
    grid_table = jnp.stack([minus_x, plus_x, minus_y, plus_y, minus_z, plus_z], axis=-1)
    inverse = jnp.argsort(orders, axis=-1).astype(jnp.int32)
    by_device = jnp.take_along_axis(grid_table, inverse[..., None], axis=2)
    return jnp.transpose(by_device, (0, 2, 1, 3)).reshape(LAYERS, SLOTS, 6).astype(jnp.int32)


def block_scale(own_key, extent, cuts, smallest, top_value):
    def one(dim, shards_of):
        steps = jax.random.uniform(jax.random.fold_in(jax.random.fold_in(own_key, 6), dim), (shards_of,), jnp.float32, smallest / len(cuts), top_value / len(cuts))
        return jnp.repeat(jnp.exp(steps), extent[dim] // shards_of).reshape((-1,) + (1,) * (len(extent) - dim - 1))

    gain = one(*cuts[0])
    for cut in cuts[1:]:
        gain = gain * one(*cut)
    return gain


def profile(count, total, most, lean):
    weights = [(1 << 20) // math.isqrt(grade ** lean) + 1 for grade in range(2, count + 1)]
    surplus, given = total - most - (count - 1), [1] * (count - 1)
    while surplus > 0:
        free = [i for i in range(count - 1) if given[i] < most]
        whole, left = sum([weights[i] for i in free]), surplus
        for i in free:
            more = min(most - given[i], max(1, left * weights[i] // whole), surplus)
            given[i] = given[i] + more
            surplus = surplus - more
    return np.array([most] + given)


def ragged(key, count, total, bound, skew):
    if count == 2:
        one = jax.random.randint(key, (), max(1, total - bound), min(bound, total - 1) + 1)
        return jnp.stack([one, total - one])
    sizes = jnp.asarray(profile(count, total, bound, skew), jnp.int32)
    couples = (count - 1) // 2
    giver, taker = sizes[1:1 + 2 * couples:2], sizes[2:2 + 2 * couples:2]
    slack = jnp.minimum(giver - 1, bound - taker)
    moved = jax.random.randint(jax.random.fold_in(key, 1), (couples,), 0, 1 << 20) % (slack + 1)
    sizes = sizes.at[1:1 + 2 * couples:2].set(giver - moved).at[2:2 + 2 * couples:2].set(taker + moved)
    return sizes[jax.random.permutation(jax.random.fold_in(key, 2), count)]


def normal_values(stream_key, shape, scale, limit, cuts=(), kind=jnp.bfloat16):
    factor_of = block_scale(stream_key, shape, cuts, -0.22, 0.18) if cuts else 1.0
    drawn = jax.random.normal(stream_key, shape, jnp.float32) * scale * factor_of
    return jnp.minimum(jnp.maximum(drawn, -limit), limit).astype(kind)


def setup_inputs(seed: int = 0) -> dict:
    seeds = jax.random.split(jax.random.key(seed), 7)
    adjoint = normal_values(seeds[0], (LAYERS, SLOTS, 19, B, B * B), 1.0, 6.0, ((0, 4), (1, 32)), jnp.float32)
    velocity = normal_values(seeds[1], (LAYERS, SLOTS, 3, B, B * B), 0.08, 0.32, ((0, 4), (1, 32)), jnp.float32)
    porosity = jnp.clip(1.0 * jax.random.uniform(seeds[2], (LAYERS, SLOTS, B, B * B), jnp.float32) ** block_scale(seeds[2], (LAYERS, SLOTS, B, B * B), ((0, 4), (1, 32)), -0.2, 0.2), 0.0, 1.0)
    block_x = draw_block_x(jax.random.fold_in(seeds[6], 71), 0)
    neighbours = draw_neighbours(jax.random.fold_in(seeds[6], 71), 0)
    owner_map = ragged(seeds[5], COLS, UNITS, MOSTU, 2).astype(jnp.int32)
    return {"adjoint": adjoint, "velocity": velocity, "porosity": porosity, "block_x": block_x, "neighbours": neighbours, "owner_map": owner_map}


VELOCITIES = np.array([[0, 0, 0], [1, 0, 0], [-1, 0, 0], [0, 1, 0], [0, -1, 0], [0, 0, 1], [0, 0, -1], [1, 1, 0], [-1, -1, 0], [1, -1, 0], [-1, 1, 0], [1, 0, 1], [-1, 0, -1], [1, 0, -1], [-1, 0, 1], [0, 1, 1], [0, -1, -1], [0, 1, -1], [0, -1, 1]], dtype=np.float32)
WEIGHTS = np.array([1.0 / 3.0] + [1.0 / 18.0] * 6 + [1.0 / 36.0] * 12, dtype=np.float32)
EAST_POPS = [1, 7, 9, 11, 13]
WEST_POPS = [2, 8, 10, 12, 14]
NORTH_POPS = [3, 7, 10, 15, 17]
SOUTH_POPS = [4, 8, 9, 16, 18]
UPPER_POPS = [5, 11, 14, 15, 18]
LOWER_POPS = [6, 12, 13, 16, 17]
RELAX_RATE = 1.25
DRAG_RATE = 0.3
FILTER_TAPS = [1.0 / 3.0, 2.0 / 3.0, 1.0, 2.0 / 3.0, 1.0 / 3.0]


def pop_table(values, rank_count, pop_axis):
    shape = [1] * rank_count
    shape[pop_axis] = values.shape[0]
    return jnp.asarray(values).reshape(shape)


def collide(state, velocity, porosity, pop_axis):
    rank_count = state.ndim
    components = [lax.index_in_dim(velocity, c, pop_axis, keepdims=True) for c in range(3)]
    lattice = [pop_table(VELOCITIES[:, c], rank_count, pop_axis) for c in range(3)]
    weights = pop_table(WEIGHTS, rank_count, pop_axis)
    speed_sq = components[0] * components[0] + components[1] * components[1] + components[2] * components[2]
    along = lattice[0] * components[0] + lattice[1] * components[1] + lattice[2] * components[2]
    weighted = weights * state
    scalar = jnp.sum(weighted * (1.0 + 3.0 * along + 4.5 * along * along - 1.5 * speed_sq), axis=pop_axis, keepdims=True)
    weight_total = jnp.sum(weighted, axis=pop_axis, keepdims=True)
    grown = weighted * (3.0 + 9.0 * along)
    vector_part = [jnp.sum(grown * lattice[c], axis=pop_axis, keepdims=True) - 3.0 * components[c] * weight_total for c in range(3)]
    momentum = [jnp.sum(lattice[c] * state, axis=pop_axis, keepdims=True) for c in range(3)]
    sens_step = components[0] * momentum[0] + components[1] * momentum[1] + components[2] * momentum[2]
    relative = [lattice[c] - components[c] for c in range(3)]
    project_vector = relative[0] * vector_part[0] + relative[1] * vector_part[1] + relative[2] * vector_part[2]
    project_momentum = relative[0] * momentum[0] + relative[1] * momentum[1] + relative[2] * momentum[2]
    collided = (1.0 - RELAX_RATE) * state + RELAX_RATE * (scalar + project_vector) - DRAG_RATE * porosity * project_momentum
    return collided, sens_step


def smooth_axis(field, axis_pos):
    length = field.shape[axis_pos]
    widths = [(0, 0)] * field.ndim
    widths[axis_pos] = (2, 2)
    padded = jnp.pad(field, widths)
    result = FILTER_TAPS[0] * lax.slice_in_dim(padded, 0, length, axis=axis_pos)
    for offset in range(1, 5):
        result = result + FILTER_TAPS[offset] * lax.slice_in_dim(padded, offset, offset + length, axis=axis_pos)
    return result


def take_slots(face, slot_index):
    count = face.shape[1]
    padded = jnp.concatenate([face, jnp.zeros_like(face[:, :1])], axis=1)
    safe = jnp.where(slot_index < 0, count, slot_index).astype(jnp.int32)
    return jax.vmap(lambda layer, picks: layer[picks])(padded, safe)


def stream(collided, neighbours):
    moved = collided
    group = moved[:, :, EAST_POPS]
    incoming = take_slots(group[..., :1], neighbours[:, :, 1])
    moved = moved.at[:, :, EAST_POPS].set(jnp.concatenate([group[..., 1:], incoming], axis=-1))
    group = moved[:, :, WEST_POPS]
    incoming = take_slots(group[..., -1:], neighbours[:, :, 0])
    moved = moved.at[:, :, WEST_POPS].set(jnp.concatenate([incoming, group[..., :-1]], axis=-1))
    group = moved[:, :, NORTH_POPS]
    incoming = take_slots(group[..., :1, :], neighbours[:, :, 3])
    moved = moved.at[:, :, NORTH_POPS].set(jnp.concatenate([group[..., 1:, :], incoming], axis=-2))
    group = moved[:, :, SOUTH_POPS]
    incoming = take_slots(group[..., -1:, :], neighbours[:, :, 2])
    moved = moved.at[:, :, SOUTH_POPS].set(jnp.concatenate([incoming, group[..., :-1, :]], axis=-2))
    group = moved[:, :, UPPER_POPS]
    face = group[..., :1, :, :]
    source = jnp.concatenate([face[1:], jnp.zeros_like(face[:1])], axis=0)
    incoming = take_slots(source, neighbours[:, :, 5])
    moved = moved.at[:, :, UPPER_POPS].set(jnp.concatenate([group[..., 1:, :, :], incoming], axis=-3))
    group = moved[:, :, LOWER_POPS]
    face = group[..., -1:, :, :]
    source = jnp.concatenate([jnp.zeros_like(face[:1]), face[:-1]], axis=0)
    incoming = take_slots(source, neighbours[:, :, 4])
    moved = moved.at[:, :, LOWER_POPS].set(jnp.concatenate([incoming, group[..., :-1, :, :]], axis=-3))
    return moved


def reference(adjoint, velocity, porosity, block_x, neighbours, owner_map):
    state = adjoint.reshape(LAYERS, SLOTS, 19, B, B, B)
    flow = velocity.reshape(LAYERS, SLOTS, 3, B, B, B)
    design = porosity.reshape(LAYERS, SLOTS, 1, B, B, B)
    sens_total = jnp.zeros((LAYERS, SLOTS, B, B, B), jnp.float32)
    for iteration in range(STEPS):
        collided, sens_step = collide(state, flow, design, 2)
        sens_total = sens_total + sens_step[:, :, 0]
        state = stream(collided, neighbours)
    columns = block_x.reshape(LAYERS, COLS, K)
    hits = columns[..., None] == jnp.arange(COLS, dtype=jnp.int32)
    holder = jnp.sum(jnp.where(hits, jnp.arange(COLS, dtype=jnp.int32)[None, :, None, None], 0), axis=1).astype(jnp.int32)
    per_device = sens_total.reshape(LAYERS, COLS, K, B, B, B)
    row_ids = jnp.arange(K, dtype=jnp.int32)[:, None]
    placed = jax.vmap(lambda source, picks: source[picks, row_ids])(per_device, holder)
    field = placed.transpose(0, 3, 1, 4, 2, 5).reshape(LAYERS * B, K * B, COLS * B)
    filtered = smooth_axis(smooth_axis(smooth_axis(field, 1), 2), 0)
    band_rows = 2 * owner_map
    band_start = jnp.cumsum(band_rows) - band_rows
    offsets = jnp.arange(ROWS, dtype=jnp.int32)
    wanted = band_start[:, None] + offsets[None, :]
    present = offsets[None, :] < band_rows[:, None]
    picked = jnp.take(filtered, jnp.clip(wanted, 0, K * B - 1).reshape(-1), axis=1)
    picked = picked.reshape(LAYERS * B, COLS, ROWS, COLS * B)
    picked = jnp.where(present[None, :, :, None], picked, jnp.zeros_like(picked))
    smoothed = picked.reshape(LAYERS, B, COLS, ROWS, COLS * B).transpose(0, 2, 3, 1, 4)
    return state.reshape(adjoint.shape), smoothed
```

```python
import functools

import jax
import jax.numpy as jnp
import numpy as np
from jax import lax
from jax.experimental import pallas as pl
from jax.experimental.pallas import tpu as pltpu
from jax.sharding import PartitionSpec as P

VEL = [
    (0, 0, 0),
    (1, 0, 0), (-1, 0, 0), (0, 1, 0), (0, -1, 0), (0, 0, 1), (0, 0, -1),
    (1, 1, 0), (-1, -1, 0), (1, -1, 0), (-1, 1, 0),
    (1, 0, 1), (-1, 0, -1), (1, 0, -1), (-1, 0, 1),
    (0, 1, 1), (0, -1, -1), (0, 1, -1), (0, -1, 1),
]
XPOPS = [1, 7, 9, 11, 13, 2, 8, 10, 12, 14]
YPOPS = [3, 7, 10, 15, 17, 4, 8, 9, 16, 18]
ZPOPS = [5, 11, 14, 15, 18, 6, 12, 13, 16, 17]
NB = 32
NZ = 4
MESH = pl.DeviceIdType.MESH


def collide(f, u, por):
    def total(parts):
        acc = parts[0]
        for part in parts[1:]:
            acc = acc + part
        return acc

    ux, uy, uz = u
    plus = lambda a, b: f[a] + f[b]
    minus = lambda a, b: f[a] - f[b]
    ax, ay, az = plus(1, 2), plus(3, 4), plus(5, 6)
    bx, by, bz = minus(1, 2), minus(3, 4), minus(5, 6)
    s78, s9a = plus(7, 8), plus(9, 10)
    d78, d9a = minus(7, 8), minus(9, 10)
    sbc, sde = plus(11, 12), plus(13, 14)
    dbc, dde = minus(11, 12), minus(13, 14)
    sfg, shi = plus(15, 16), plus(17, 18)
    dfg, dhi = minus(15, 16), minus(17, 18)
    dx = (d78 + d9a) + (dbc + dde)
    dy = (d78 - d9a) + (dfg + dhi)
    dz = (dbc - dde) + (dfg - dhi)
    momx, momy, momz = bx + dx, by + dy, bz + dz
    w1, w2 = 1.0 / 18.0, 1.0 / 36.0
    gx = w1 * bx + w2 * dx
    gy = w1 * by + w2 * dy
    gz = w1 * bz + w2 * dz
    xy, xz, yz = s78 + s9a, sbc + sde, sfg + shi
    qxx = w1 * ax + w2 * (xy + xz)
    qyy = w1 * ay + w2 * (xy + yz)
    qzz = w1 * az + w2 * (xz + yz)
    qxy = w2 * (s78 - s9a)
    qxz = w2 * (sbc - sde)
    qyz = w2 * (sfg - shi)
    weight = (1.0 / 3.0) * f[0] + w1 * (ax + ay + az) + w2 * (xy + xz + yz)
    qux = qxx * ux + qxy * uy + qxz * uz
    quy = qxy * ux + qyy * uy + qyz * uz
    quz = qxz * ux + qyz * uy + qzz * uz
    uu = ux * ux + uy * uy + uz * uz
    ug = ux * gx + uy * gy + uz * gz
    uqu = ux * qux + uy * quy + uz * quz
    um = ux * momx + uy * momy + uz * momz
    scalar = weight * (1.0 - 1.5 * uu) + 3.0 * ug + 4.5 * uqu
    uv = 3.0 * ug + 9.0 * uqu - 3.0 * uu * weight
    drag = 0.3 * por
    base = 1.25 * (scalar - uv) + drag * um
    ex = 1.25 * (3.0 * gx + 9.0 * qux - 3.0 * ux * weight) - drag * momx
    ey = 1.25 * (3.0 * gy + 9.0 * quy - 3.0 * uy * weight) - drag * momy
    ez = 1.25 * (3.0 * gz + 9.0 * quz - 3.0 * uz * weight) - drag * momz
    e = (ex, ey, ez)
    post = []
    for i, c in enumerate(VEL):
        acc = base - 0.25 * f[i]
        for axis in range(3):
            if c[axis] == 1:
                acc = acc + e[axis]
            elif c[axis] == -1:
                acc = acc - e[axis]
        post.append(acc)
    return post, um


def kernel(
    adj, vel, por, nbv, nbs, bx, om, out, smo,
    post, sens, sa, ra, rza, ob, obz, rb, pm, shifted, ss, rs, fld, flt, hs, hr,
    asend, arecv, zsend, zrecv, bsend, brecv, csend, crecv, ssend, srecv, hsend, hrecv,
):
    me = lax.axis_index("blk")
    layer = lax.axis_index("gz")
    up, down = lax.rem(layer + 1, NZ), lax.rem(layer + NZ - 1, NZ)
    f32 = jnp.float32

    barrier = pltpu.get_barrier_semaphore()

    def hello(d, carry):
        peer = lax.rem(me + d, NB)
        pl.semaphore_signal(barrier, inc=1, device_id={"blk": peer, "gz": layer}, device_id_type=MESH)
        return carry

    lax.fori_loop(1, NB, hello, 0)
    pl.semaphore_signal(barrier, inc=1, device_id={"blk": me, "gz": up}, device_id_type=MESH)
    pl.semaphore_signal(barrier, inc=1, device_id={"blk": me, "gz": down}, device_id_type=MESH)

    def hello_up(d, carry):
        pl.semaphore_signal(barrier, inc=1, device_id={"blk": d, "gz": up}, device_id_type=MESH)
        return carry

    def hello_down(d, carry):
        pl.semaphore_signal(barrier, inc=1, device_id={"blk": d, "gz": down}, device_id_type=MESH)
        return carry

    @pl.when((me >= 16) & (me < 21))
    def _():
        lax.fori_loop(0, NB, hello_up, 0)

    @pl.when((me >= 21) & (me < 26))
    def _():
        lax.fori_loop(0, NB, hello_down, 0)

    lane = lax.broadcasted_iota(jnp.int32, (1, 256), 1)
    lane_x, lane_y = lane % 16, lane // 16
    depth = lax.broadcasted_iota(jnp.int32, (16, 1), 0)

    def collide_all(src, step):
        def body(t, carry):
            k, half = t // 2, t % 2
            rows = pl.ds(pl.multiple_of(half * 8, 8), 8)
            f = [src[0, k, i, rows, :] for i in range(19)]
            u = [vel[0, k, c, rows, :] for c in range(3)]
            new, um = collide(f, u, por[0, k, rows, :])
            for i in range(19):
                post[k, i, rows, :] = new[i]
            if step == 0:
                sens[k, rows, :] = um
            else:
                sens[k, rows, :] = sens[k, rows, :] + um
            return carry

        lax.fori_loop(0, 16, body, 0)

    def pack_all(step):
        def body(k, carry):
            rec = jnp.zeros((16, 256), f32)
            for j, i in enumerate(XPOPS):
                cx, cy, cz = VEL[i]
                a = post[k, i]
                if cz:
                    a = pltpu.roll(a, (-cz) % 16, 0)
                x0 = 0 if cx == 1 else 15
                s = (j - x0 - 16 * cy) % 256
                if s:
                    a = pltpu.roll(a, s, 1)
                rec = jnp.where(lane_x == j, a, rec)
            sa[step, pl.ds(k, 16, stride=16), :] = rec[:, :128]
            sa[step, pl.ds(k + 8, 16, stride=16), :] = rec[:, 128:]
            rec = jnp.zeros((16, 256), f32)
            for j, i in enumerate(YPOPS):
                cx, cy, cz = VEL[i]
                a = post[k, i]
                if cz:
                    a = pltpu.roll(a, (-cz) % 16, 0)
                y0 = 0 if cy == 1 else 15
                s = ((j - y0) * 16 - cx) % 256
                if s:
                    a = pltpu.roll(a, s, 1)
                rec = jnp.where(lane_y == j, a, rec)
            sa[step, pl.ds(k + 256, 16, stride=16), :] = rec[:, :128]
            sa[step, pl.ds(k + 264, 16, stride=16), :] = rec[:, 128:]
            for j, i in enumerate(ZPOPS):
                z0 = 0 if VEL[i][2] == 1 else 15
                row = post[k, i, pl.ds(z0, 1), :]
                sa[step, pl.ds((32 + j) * 16 + k, 1), :] = row[:, :128]
                sa[step, pl.ds((32 + j) * 16 + 8 + k, 1), :] = row[:, 128:]
            return carry

        lax.fori_loop(0, 8, body, 0)
        for j, i in enumerate(ZPOPS):
            cx, cy, _ = VEL[i]
            if cx == 0 and cy == 0:
                continue
            base = (32 + j) * 16
            a = jnp.concatenate([sa[step, base:base + 8, :], sa[step, base + 8:base + 16, :]], axis=1)
            if cx == 1:
                a = jnp.where(lane_x == 15, pltpu.roll(a, 15, 1), pltpu.roll(a, 255, 1))
            elif cx == -1:
                a = jnp.where(lane_x == 0, pltpu.roll(a, 241, 1), pltpu.roll(a, 1, 1))
            else:
                a = pltpu.roll(a, (-16 * cy) % 256, 1)
            sa[step, base:base + 8, :] = a[:, :128]
            sa[step, base + 8:base + 16, :] = a[:, 128:]

    def stream_all(step):
        def body(k, carry):
            half = lambda first: jnp.concatenate(
                [rb[step, pl.ds(first + k, 16, stride=16), :], rb[step, pl.ds(first + 8 + k, 16, stride=16), :]],
                axis=1,
            )
            rx, ry = half(0), half(256)
            for i, (cx, cy, cz) in enumerate(VEL):
                a = post[k, i]
                s = (-(16 * cy + cx)) % 256
                if s:
                    a = pltpu.roll(a, s, 1)
                if cz:
                    a = pltpu.roll(a, (-cz) % 16, 0)
                if cy:
                    j = YPOPS.index(i)
                    yt = 15 if cy == 1 else 0
                    s = ((yt - j) * 16) % 256
                    face = pltpu.roll(ry, s, 1) if s else ry
                    a = jnp.where(lane_y == yt, face, a)
                if cx:
                    j = XPOPS.index(i)
                    xt = 15 if cx == 1 else 0
                    s = (xt - j) % 256
                    face = pltpu.roll(rx, s, 1) if s else rx
                    a = jnp.where(lane_x == xt, face, a)
                if cz:
                    j = ZPOPS.index(i)
                    zt = 15 if cz == 1 else 0
                    first = (32 + j) * 16
                    row = jnp.concatenate(
                        [rb[step, pl.ds(first + k, 1), :], rb[step, pl.ds(first + 8 + k, 1), :]], axis=1
                    )
                    a = jnp.where(depth == zt, row, a)
                out[0, k, i] = a
            return carry

        lax.fori_loop(0, 8, body, 0)

    def remote(src, dst, send, recv, blk, gz):
        return pltpu.make_async_remote_copy(
            src_ref=src, dst_ref=dst, send_sem=send, recv_sem=recv,
            device_id={"blk": blk, "gz": gz}, device_id_type=MESH,
        )

    def send_a(step):
        def body(d, carry):
            peer = lax.rem(me + d, NB)
            rows = pl.ds(pl.multiple_of(peer * 16, 16), 16)
            remote(sa.at[step, rows], ra.at[step, me], asend.at[step], arecv.at[step], peer, layer).start()
            return carry

        def body_z(j, carry):
            rows = pl.ds(pl.multiple_of((32 + j) * 16, 16), 16)
            dest = jnp.where(j < 5, down, up)
            remote(sa.at[step, rows], rza.at[step, me], zsend.at[step], zrecv.at[step], 16 + j, dest).start()
            return carry

        lax.fori_loop(0, 10, body_z, 0)
        lax.fori_loop(1, NB, body, 0)
        ra[step, me] = sa[step, pl.ds(pl.multiple_of(me * 16, 16), 16), :]

    def split3(v):
        hi = v.astype(jnp.bfloat16)
        rest = v - hi.astype(f32)
        mid = rest.astype(jnp.bfloat16)
        low = (rest - mid.astype(f32)).astype(jnp.bfloat16)
        return hi, mid, low

    def pick(d, v):
        p = pm[d]
        hi, mid, low = split3(v)
        dot = lambda part: jnp.dot(p, part, preferred_element_type=f32)
        return (dot(hi) + dot(mid)) + dot(low)

    def whole(ref, step):
        return jnp.concatenate(
            [ref[step, :, 0:8, :].reshape(256, 128), ref[step, :, 8:16, :].reshape(256, 128)], axis=1
        )

    def put(ref, step, v):
        ref[step, :, 0:8, :] = v[:, :128].reshape(NB, 8, 128)
        ref[step, :, 8:16, :] = v[:, 128:].reshape(NB, 8, 128)

    def wait_bytes(ref, sem):
        pltpu.make_async_copy(ref, ref, sem).wait()

    is_z = (me >= 16) & (me < 26)

    def middle(step):
        wait_bytes(ra.at[step, pl.ds(0, NB - 1)], arecv.at[step])

        @pl.when(me < 16)
        def _():
            v = whole(ra, step)
            north = (lane_y == 15) & ((lane_x == 1) | (lane_x == 7))
            south = (lane_y == 0) & ((lane_x == 2) | (lane_x == 6))
            fix = pick(3, jnp.where(north, v, 0.0)) + pick(2, jnp.where(south, v, 0.0))
            v = jnp.where(north | south, fix, v)
            put(ob, step, pick(1, jnp.where(lane_x < 5, v, 0.0)) + pick(0, jnp.where(lane_x >= 5, v, 0.0)))

        @pl.when(me >= 16)
        def _():
            v = whole(ra, step)
            put(ob, step, pick(3, jnp.where(lane_y < 5, v, 0.0)) + pick(2, jnp.where(lane_y >= 5, v, 0.0)))

        def body(d, carry):
            peer = lax.rem(me + d, NB)
            rows = pl.ds(pl.multiple_of(me * 16, 16), 16)
            remote(ob.at[step, peer], rb.at[step, rows], bsend.at[step], brecv.at[step], peer, layer).start()
            return carry

        lax.fori_loop(1, NB, body, 0)
        rb[step, pl.ds(pl.multiple_of(me * 16, 16), 16), :] = ob[step, me]

        @pl.when(is_z)
        def _():
            wait_bytes(rza.at[step], zrecv.at[step])
            j = me - 16
            a = pick(jnp.where(j < 5, 5, 4), whole(rza, step))
            on_x = (j == 1) | (j == 2) | (j == 6) | (j == 7)
            plus = (j == 1) | (j == 3) | (j == 7) | (j == 9)
            axial = (j == 0) | (j == 5)
            where = jnp.where(plus, 15, 0)
            hit = jnp.where(on_x, lane_x, lane_y) == jnp.where(axial, -1, where)
            side = jnp.where(on_x, 0, 2) + jnp.where(plus, 1, 0)
            put(obz, step, jnp.where(hit, pick(side, a), a))

            def body(d, carry):
                peer = lax.rem(me + d, NB)
                rows = pl.ds(pl.multiple_of((me + 16) * 16, 16), 16)
                remote(obz.at[step, peer], rb.at[step, rows], csend.at[step], crecv.at[step], peer, layer).start()
                return carry

            lax.fori_loop(1, NB, body, 0)
            rb[step, pl.ds(pl.multiple_of((me + 16) * 16, 16), 16), :] = obz[step, me]

    def receive_b(step):
        wait_bytes(rb.at[step, pl.ds(0, 31 * 16)], brecv.at[step])

        @pl.when(is_z)
        def _():
            wait_bytes(rb.at[step, pl.ds(0, 9 * 16)], crecv.at[step])

        @pl.when(jnp.logical_not(is_z))
        def _():
            wait_bytes(rb.at[step, pl.ds(0, 10 * 16)], crecv.at[step])

    collide_all(adj, 0)
    pack_all(0)
    pl.semaphore_wait(barrier, (NB - 1) + 2 + 10)
    send_a(0)

    @pl.loop(0, 256, step=32)
    def _(t):
        rows = pl.ds(pl.multiple_of(t, 32), 32)
        column = lax.broadcasted_iota(jnp.int32, (32, 256), 1)
        table = nbv[0, rows, :]
        for d in range(6):
            pm[d, rows, :] = jnp.where(table[:, d:d + 1] == column, 1.0, 0.0).astype(jnp.bfloat16)

    middle(0)
    receive_b(0)
    stream_all(0)

    collide_all(out, 1)
    pack_all(1)
    send_a(1)

    zero = jnp.zeros((16, 128), f32)
    lane128 = lax.broadcasted_iota(jnp.int32, (1, 128), 1)

    def tile(t):
        return sens[t // 2, :, (t % 2) * 128:(t % 2) * 128 + 128] if 0 <= t < 16 else zero

    for t in range(17):
        before, here, after = tile(t - 1), tile(t), tile(t + 1)
        shifted[0, t] = jnp.where(lane128 < 32, pltpu.roll(before, 32, 1), pltpu.roll(here, 32, 1))
        shifted[1, t] = here
        shifted[2, t] = jnp.where(lane128 < 96, pltpu.roll(here, 96, 1), pltpu.roll(after, 96, 1))
        shifted[3, t] = jnp.where(lane128 < 64, pltpu.roll(here, 64, 1), pltpu.roll(after, 64, 1))

    def cut(j, pairs):
        s, t = pairs % 4, pairs // 4
        ss[j, :, :128] = shifted[s, t]
        ss[j, :, 128:] = shifted[s, t + 1]
        return pairs + om[j]

    lax.fori_loop(0, NB, cut, jnp.int32(0))

    def send_rows(d, carry):
        peer = lax.rem(me + d, NB)
        remote(ss.at[peer], rs.at[me], ssend, srecv, peer, layer).start()
        return carry

    lax.fori_loop(1, NB, send_rows, 0)
    rs[me] = ss[me]

    middle(1)

    wait_bytes(rs.at[pl.ds(0, NB - 1)], srecv)
    first = 2 * lax.fori_loop(0, NB, lambda i, acc: acc + jnp.where(i < me, om[i], 0), jnp.int32(0))
    own_rows = 2 * om[me]
    kf = (first + 14) // 16 - 1
    split = 16 * (kf + 1) - (first - 2)
    ka, kb = jnp.maximum(kf, 0), jnp.minimum(kf + 1, 7)

    def find(a, carry):
        ta, tb = carry
        ta = jnp.where(bx[0, a * 8 + ka] == 0, a * 8 + ka, ta)
        tb = jnp.where(bx[0, a * 8 + kb] == 0, a * 8 + kb, tb)
        return ta, tb

    start = lax.fori_loop(0, NB, find, (jnp.int32(0), jnp.int32(0)))
    group = lane128 // 16

    def arrange(cg, carry):
        ta, tb = carry
        parts = []
        for _ in range(8):
            parts.append(jnp.where(lane_y < split, rs[ta // 8], rs[tb // 8]))
            ta = jnp.maximum(nbs[0, ta, 1], 0)
            tb = jnp.maximum(nbs[0, tb, 1], 0)
        for r in range(16):
            h = r // 8
            acc = None
            for c in range(8):
                a = parts[c][:, h * 128:h * 128 + 128]
                s = ((c - r % 8) * 16) % 128
                if s:
                    a = pltpu.roll(a, s, 1)
                acc = a if acc is None else jnp.where(group == c, a, acc)
            fld[cg, r] = acc
        return ta, tb

    lax.fori_loop(0, 4, arrange, start)

    lane512 = lax.broadcasted_iota(jnp.int32, (1, 512), 1)
    third = 1.0 / 3.0

    def taps(a, b, c, d, e):
        return third * (a + e) + (2.0 * third) * (b + d) + c

    for r in range(12):
        row = lambda q: jnp.concatenate([fld[cg, q] for cg in range(4)], axis=1)
        v = taps(row(r), row(r + 1), row(r + 2), row(r + 3), row(r + 4))
        m2 = jnp.where(lane512 >= 2, pltpu.roll(v, 2, 1), 0.0)
        m1 = jnp.where(lane512 >= 1, pltpu.roll(v, 1, 1), 0.0)
        p1 = jnp.where(lane512 < 511, pltpu.roll(v, 511, 1), 0.0)
        p2 = jnp.where(lane512 < 510, pltpu.roll(v, 510, 1), 0.0)
        v = taps(m2, m1, v, p1, p2)
        flt[r] = v
        hs[0, 2 * r:2 * r + 2, :] = v[0:2, :]
        hs[1, 2 * r:2 * r + 2, :] = v[14:16, :]

    to_down = remote(hs.at[0], hr.at[1], hsend.at[0], hrecv.at[1], me, down)
    to_up = remote(hs.at[1], hr.at[0], hsend.at[1], hrecv.at[0], me, up)
    to_down.start()
    to_up.start()

    receive_b(1)
    stream_all(1)

    to_down.wait_send()
    to_up.wait_send()
    to_up.wait_recv()
    to_down.wait_recv()
    below = jnp.where(layer > 0, 1.0, 0.0)
    above = jnp.where(layer < NZ - 1, 1.0, 0.0)
    for r in range(12):
        v = jnp.concatenate(
            [hr[0, 2 * r:2 * r + 2, :] * below, flt[r], hr[1, 2 * r:2 * r + 2, :] * above], axis=0
        )
        v = taps(v[0:16], v[1:17], v[2:18], v[3:19], v[4:20])
        smo[0, 0, r] = jnp.where(own_rows > r, v, 0.0)

    for step in range(2):
        wait_bytes(sa.at[step, pl.ds(0, 31 * 16)], asend.at[step])
        wait_bytes(sa.at[step, pl.ds(0, 10 * 16)], zsend.at[step])
        wait_bytes(ob.at[step, pl.ds(0, NB - 1)], bsend.at[step])

        @pl.when(is_z)
        def _():
            wait_bytes(obz.at[step, pl.ds(0, NB - 1)], csend.at[step])

    wait_bytes(ss.at[pl.ds(0, NB - 1)], ssend)


def local(adjoint, velocity, porosity, block_x, neighbours, owner_map):
    f32 = jnp.float32
    vmem = pl.BlockSpec(memory_space=pltpu.VMEM)
    smem = pl.BlockSpec(memory_space=pltpu.SMEM)
    dma = pltpu.SemaphoreType.DMA
    return pl.pallas_call(
        kernel,
        out_shape=(
            jax.ShapeDtypeStruct((1, 8, 19, 16, 256), f32),
            jax.ShapeDtypeStruct((1, 1, 12, 16, 512), f32),
        ),
        in_specs=[vmem, vmem, vmem, vmem, smem, smem, smem],
        out_specs=(vmem, vmem),
        scratch_shapes=[
            pltpu.VMEM((8, 19, 16, 256), f32),
            pltpu.VMEM((8, 16, 256), f32),
            pltpu.VMEM((2, 42 * 16, 128), f32),
            pltpu.VMEM((2, NB, 16, 128), f32),
            pltpu.VMEM((2, NB, 16, 128), f32),
            pltpu.VMEM((2, NB, 16, 128), f32),
            pltpu.VMEM((2, NB, 16, 128), f32),
            pltpu.VMEM((2, 42 * 16, 128), f32),
            pltpu.VMEM((6, 256, 256), jnp.bfloat16),
            pltpu.VMEM((4, 17, 16, 128), f32),
            pltpu.VMEM((NB, 16, 256), f32),
            pltpu.VMEM((NB, 16, 256), f32),
            pltpu.VMEM((4, 16, 16, 128), f32),
            pltpu.VMEM((12, 16, 512), f32),
            pltpu.VMEM((2, 24, 512), f32),
            pltpu.VMEM((2, 24, 512), f32),
            dma((2,)), dma((2,)),
            dma((2,)), dma((2,)),
            dma((2,)), dma((2,)),
            dma((2,)), dma((2,)),
            dma, dma,
            dma((2,)), dma((2,)),
        ],
        compiler_params=pltpu.CompilerParams(
            collective_id=0, has_side_effects=True, vmem_limit_bytes=48 * 1024 * 1024
        ),
    )(adjoint, velocity, porosity, neighbours, neighbours, block_x, owner_map)


def solution(mesh):
    placed = (
        P("gz", "blk", None, None, None),
        P("gz", "blk", None, None, None),
        P("gz", "blk", None, None),
        P("gz", None),
        P("gz", None, None),
        P(),
    )
    return jax.shard_map(
        local,
        mesh=mesh,
        in_specs=placed,
        out_specs=(P("gz", "blk", None, None, None), P("gz", "blk", None, None, None)),
        check_vma=False,
    )
```

```python
import functools

import jax
import jax.numpy as jnp
import numpy as np
from jax import lax
from jax.experimental import pallas as pl
from jax.experimental.pallas import tpu as pltpu
from jax.sharding import PartitionSpec as P

VEL = [
    (0, 0, 0),
    (1, 0, 0), (-1, 0, 0), (0, 1, 0), (0, -1, 0), (0, 0, 1), (0, 0, -1),
    (1, 1, 0), (-1, -1, 0), (1, -1, 0), (-1, 1, 0),
    (1, 0, 1), (-1, 0, -1), (1, 0, -1), (-1, 0, 1),
    (0, 1, 1), (0, -1, -1), (0, 1, -1), (0, -1, 1),
]
XPOPS = [1, 7, 9, 11, 13, 2, 8, 10, 12, 14]
YPOPS = [3, 7, 10, 15, 17, 4, 8, 9, 16, 18]
ZPOPS = [5, 11, 14, 15, 18, 6, 12, 13, 16, 17]
NB = 32
NZ = 4
MESH = pl.DeviceIdType.MESH


def collide(f, u, por):
    def total(parts):
        acc = parts[0]
        for part in parts[1:]:
            acc = acc + part
        return acc

    ux, uy, uz = u
    plus = lambda a, b: f[a] + f[b]
    minus = lambda a, b: f[a] - f[b]
    ax, ay, az = plus(1, 2), plus(3, 4), plus(5, 6)
    bx, by, bz = minus(1, 2), minus(3, 4), minus(5, 6)
    s78, s9a = plus(7, 8), plus(9, 10)
    d78, d9a = minus(7, 8), minus(9, 10)
    sbc, sde = plus(11, 12), plus(13, 14)
    dbc, dde = minus(11, 12), minus(13, 14)
    sfg, shi = plus(15, 16), plus(17, 18)
    dfg, dhi = minus(15, 16), minus(17, 18)
    dx = (d78 + d9a) + (dbc + dde)
    dy = (d78 - d9a) + (dfg + dhi)
    dz = (dbc - dde) + (dfg - dhi)
    momx, momy, momz = bx + dx, by + dy, bz + dz
    w1, w2 = 1.0 / 18.0, 1.0 / 36.0
    gx = w1 * bx + w2 * dx
    gy = w1 * by + w2 * dy
    gz = w1 * bz + w2 * dz
    xy, xz, yz = s78 + s9a, sbc + sde, sfg + shi
    qxx = w1 * ax + w2 * (xy + xz)
    qyy = w1 * ay + w2 * (xy + yz)
    qzz = w1 * az + w2 * (xz + yz)
    qxy = w2 * (s78 - s9a)
    qxz = w2 * (sbc - sde)
    qyz = w2 * (sfg - shi)
    weight = (1.0 / 3.0) * f[0] + w1 * (ax + ay + az) + w2 * (xy + xz + yz)
    qux = qxx * ux + qxy * uy + qxz * uz
    quy = qxy * ux + qyy * uy + qyz * uz
    quz = qxz * ux + qyz * uy + qzz * uz
    uu = ux * ux + uy * uy + uz * uz
    ug = ux * gx + uy * gy + uz * gz
    uqu = ux * qux + uy * quy + uz * quz
    um = ux * momx + uy * momy + uz * momz
    scalar = weight * (1.0 - 1.5 * uu) + 3.0 * ug + 4.5 * uqu
    uv = 3.0 * ug + 9.0 * uqu - 3.0 * uu * weight
    drag = 0.3 * por
    base = 1.25 * (scalar - uv) + drag * um
    ex = 1.25 * (3.0 * gx + 9.0 * qux - 3.0 * ux * weight) - drag * momx
    ey = 1.25 * (3.0 * gy + 9.0 * quy - 3.0 * uy * weight) - drag * momy
    ez = 1.25 * (3.0 * gz + 9.0 * quz - 3.0 * uz * weight) - drag * momz
    e = (ex, ey, ez)
    post = []
    for i, c in enumerate(VEL):
        acc = base - 0.25 * f[i]
        for axis in range(3):
            if c[axis] == 1:
                acc = acc + e[axis]
            elif c[axis] == -1:
                acc = acc - e[axis]
        post.append(acc)
    return post, um


MOVES = [
    (5, 0, 10, 10, 15), (5, 1, 4, 10, 13), (6, 1, 14, 14, 15), (6, 2, 8, 10, 15),
    (6, 3, 2, 10, 11), (7, 3, 12, 12, 15), (7, 4, 6, 10, 15),
]


def kernel(
    adj, vel, por, nbt, bx, om, out, smo,
    velv, porv, nbv, nbx, bxs, oms, cols,
    post, sens, sa, ra, ob, rb, pm, shifted, ss, rs, fld, flt, hs, hr,
    lsem, tsem, asend, arecv, zsend, bsend, brecv, ssend, srecv, hsend, hrecv,
):
    me = lax.axis_index("blk")
    layer = lax.axis_index("gz")
    up, down = lax.rem(layer + 1, NZ), lax.rem(layer + NZ - 1, NZ)
    f32 = jnp.float32

    barrier = pltpu.get_barrier_semaphore()

    def signal(blk, gz):
        pl.semaphore_signal(barrier, inc=1, device_id={"blk": blk, "gz": gz}, device_id_type=MESH)

    def hello(d, carry):
        signal(lax.rem(me + d, NB), layer)
        return carry

    def hello_up(d, carry):
        signal(d, up)
        return carry

    def hello_down(d, carry):
        signal(d, down)
        return carry

    is_z = (me >= 20) & (me < 30)

    @pl.when((me >= 20) & (me < 25))
    def _():
        lax.fori_loop(0, NB, hello_up, 0)

    @pl.when((me >= 25) & (me < 30))
    def _():
        lax.fori_loop(0, NB, hello_down, 0)

    lax.fori_loop(1, NB, hello, 0)
    signal(me, up)
    signal(me, down)

    def loads(k):
        return (
            pltpu.make_async_copy(adj.at[0, k], out.at[0, k], lsem.at[0, k]),
            pltpu.make_async_copy(vel.at[0, k], velv.at[k], lsem.at[1, k]),
            pltpu.make_async_copy(por.at[0, k], porv.at[k], lsem.at[2, k]),
        )

    def load(k, carry):
        for copy in loads(k):
            copy.start()
        return carry

    lax.fori_loop(0, 8, load, 0)
    tables = (
        pltpu.make_async_copy(nbt, nbv, tsem.at[0]),
        pltpu.make_async_copy(nbt.at[1], nbx, tsem.at[1]),
        pltpu.make_async_copy(bx, bxs, tsem.at[2]),
        pltpu.make_async_copy(om, oms, tsem.at[3]),
    )
    for copy in tables:
        copy.start()

    lane = lax.broadcasted_iota(jnp.int32, (1, 256), 1)
    lane_x, lane_y = lane % 16, lane // 16
    depth = lax.broadcasted_iota(jnp.int32, (16, 1), 0)
    depth8 = depth % 8

    def collide_all(step):
        def body(k, carry):
            if step == 0:
                for copy in loads(k):
                    copy.wait()
            for half in range(2):
                rows = pl.ds(half * 8, 8)
                f = [out[0, k, i, rows, :] for i in range(19)]
                u = [velv[k, c, rows, :] for c in range(3)]
                new, um = collide(f, u, porv[k, rows, :])
                for i in range(19):
                    post[k, i, rows, :] = new[i]
                if step == 0:
                    sens[k, rows, :] = um
                else:
                    sens[k, rows, :] = sens[k, rows, :] + um
            return carry

        lax.fori_loop(0, 8, body, 0)

    def fold(rec, slot, width):
        turned = {n: pltpu.roll(rec, 16 - n, 0) for n in (3, 4, 5)}
        for z, q, s, low, high in MOVES:
            here = (depth8 == q) & (slot >= low) & (slot <= high)
            rec = jnp.where(here, pltpu.roll(turned[z - q], s * width, 1), rec)
        return rec

    def unfold(rec, slot, width):
        turned = {n: pltpu.roll(rec, n, 0) for n in (3, 4, 5)}
        for z, q, s, low, high in MOVES:
            here = (depth8 == z) & (slot >= low - s) & (slot <= high - s)
            rec = jnp.where(here, pltpu.roll(turned[z - q], 256 - s * width, 1), rec)
        return rec

    def pack_x(step):
        def body(k, carry):
            rec = jnp.zeros((16, 256), f32)
            for j, i in enumerate(XPOPS):
                cx, cy, cz = VEL[i]
                a = post[k, i]
                if cz:
                    a = pltpu.roll(a, (-cz) % 16, 0)
                x0 = 0 if cx == 1 else 15
                s = (j - x0 - 16 * cy) % 256
                if s:
                    a = pltpu.roll(a, s, 1)
                rec = jnp.where(lane_x == j, a, rec)
            rec = fold(rec, lane_x, 1)
            sa[step, pl.ds(k, 16, stride=16), :] = rec[:, :128]
            sa[step, pl.ds(k + 8, 16, stride=16), :] = rec[:, 128:]
            return carry

        lax.fori_loop(0, 8, body, 0)

    def pack_y(step):
        def body(k, carry):
            rec = jnp.zeros((16, 256), f32)
            for j, i in enumerate(YPOPS):
                cx, cy, cz = VEL[i]
                a = post[k, i]
                if cz:
                    a = pltpu.roll(a, (-cz) % 16, 0)
                y0 = 0 if cy == 1 else 15
                s = ((j - y0) * 16 - cx) % 256
                if s:
                    a = pltpu.roll(a, s, 1)
                rec = jnp.where(lane_y == j, a, rec)
            rec = fold(rec, lane_y, 16)
            sa[step, pl.ds(k + 256, 16, stride=16), :] = rec[:, :128]
            sa[step, pl.ds(k + 264, 16, stride=16), :] = rec[:, 128:]
            return carry

        lax.fori_loop(0, 8, body, 0)

    def pack_z(step):
        for j, i in enumerate(ZPOPS):
            cx, cy, cz = VEL[i]
            z0 = 0 if cz == 1 else 15
            a = jnp.concatenate([post[k, i, z0:z0 + 1, :] for k in range(8)], axis=0)
            if cx == 1:
                a = jnp.where(lane_x == 15, pltpu.roll(a, 15, 1), pltpu.roll(a, 255, 1))
            elif cx == -1:
                a = jnp.where(lane_x == 0, pltpu.roll(a, 241, 1), pltpu.roll(a, 1, 1))
            elif cy:
                a = pltpu.roll(a, (-16 * cy) % 256, 1)
            base = (32 + j) * 16
            sa[step, base:base + 8, :] = a[:, :128]
            sa[step, base + 8:base + 16, :] = a[:, 128:]

    def shift_all():
        def body(k, carry):
            for i, (cx, cy, cz) in enumerate(VEL):
                a = post[k, i]
                s = (-(16 * cy + cx)) % 256
                if s:
                    a = pltpu.roll(a, s, 1)
                if cz:
                    a = pltpu.roll(a, (-cz) % 16, 0)
                out[0, k, i] = a
            return carry

        lax.fori_loop(0, 8, body, 0)

    def insert_all(step):
        def body(k, carry):
            half = lambda first: jnp.concatenate(
                [rb[step, pl.ds(first + k, 16, stride=16), :], rb[step, pl.ds(first + 8 + k, 16, stride=16), :]],
                axis=1,
            )
            rx = unfold(half(0), lane_x, 1)
            ry = unfold(half(256), lane_y, 16)
            for i, (cx, cy, cz) in enumerate(VEL):
                if cx or cy:
                    a = out[0, k, i]
                    if cy:
                        j = YPOPS.index(i)
                        yt = 15 if cy == 1 else 0
                        s = ((yt - j) * 16) % 256
                        face = pltpu.roll(ry, s, 1) if s else ry
                        a = jnp.where(lane_y == yt, face, a)
                    if cx:
                        j = XPOPS.index(i)
                        xt = 15 if cx == 1 else 0
                        s = (xt - j) % 256
                        face = pltpu.roll(rx, s, 1) if s else rx
                        a = jnp.where(lane_x == xt, face, a)
                    out[0, k, i] = a
                if cz:
                    j = ZPOPS.index(i)
                    zt = 15 if cz == 1 else 0
                    first = (32 + j) * 16
                    out[0, k, i, zt:zt + 1, :128] = rb[step, pl.ds(first + k, 1), :]
                    out[0, k, i, zt:zt + 1, 128:] = rb[step, pl.ds(first + 8 + k, 1), :]
            return carry

        lax.fori_loop(0, 8, body, 0)

    def remote(src, dst, send, recv, blk, gz):
        return pltpu.make_async_remote_copy(
            src_ref=src, dst_ref=dst, send_sem=send, recv_sem=recv,
            device_id={"blk": blk, "gz": gz}, device_id_type=MESH,
        )

    def wait_bytes(ref, sem):
        pltpu.make_async_copy(ref, ref, sem).wait()

    def row_of(p):
        return jnp.where(p < 20, p // 5 * 8 + p % 5, p + 12) * 16

    def rows_of(p):
        return pl.ds(pl.multiple_of(row_of(p), 16), 16)

    def send_z(step):
        def body(j, carry):
            rows = pl.ds(pl.multiple_of((32 + j) * 16, 16), 16)
            dest = jnp.where(j < 5, down, up)
            remote(sa.at[step, rows], ra.at[step, me], zsend.at[step], arecv.at[step], 20 + j, dest).start()
            return carry

        lax.fori_loop(0, 10, body, 0)

    def send_ten(step, first):
        def body(d, carry):
            peer = first + lax.rem(me + d, 10)
            remote(
                sa.at[step, rows_of(peer)], ra.at[step, me], asend.at[step], arecv.at[step], peer, layer
            ).start()
            return carry

        mine = (me >= first) & (me < first + 10)

        @pl.when(mine)
        def _():
            ra[step, me] = sa[step, rows_of(me), :]
            lax.fori_loop(1, 10, body, 0)

        @pl.when(jnp.logical_not(mine))
        def _():
            lax.fori_loop(0, 10, body, 0)

    def split3(v):
        hi = v.astype(jnp.bfloat16)
        rest = v - hi.astype(f32)
        mid = rest.astype(jnp.bfloat16)
        low = (rest - mid.astype(f32)).astype(jnp.bfloat16)
        return hi, mid, low

    def pick(d, v):
        p = pm[d]
        hi, mid, low = split3(v)
        dot = lambda part: jnp.dot(p, part, preferred_element_type=f32)
        return (dot(hi) + dot(mid)) + dot(low)

    def whole(step):
        return jnp.concatenate(
            [ra[step, :, 0:8, :].reshape(256, 128), ra[step, :, 8:16, :].reshape(256, 128)], axis=1
        )

    def put(step, v):
        ob[step, :, 0:8, :] = v[:, :128].reshape(NB, 8, 128)
        ob[step, :, 8:16, :] = v[:, 128:].reshape(NB, 8, 128)

    def middle(step):
        turn = me % 5 * 6

        @pl.when(me < 20)
        def _():
            wait_bytes(ra.at[step, pl.ds(0, NB - 1)], arecv.at[step])

        @pl.when(is_z)
        def _():
            wait_bytes(ra.at[step], arecv.at[step])

        @pl.when(me < 10)
        def _():
            v = whole(step)
            item = jnp.where(lane_x < 10, lane_x, (lane_x + turn - 10) % 10)
            north = (lane_y == 15) & ((item == 1) | (item == 7))
            south = (lane_y == 0) & ((item == 2) | (item == 6))
            fix = pick(3, jnp.where(north, v, 0.0)) + pick(2, jnp.where(south, v, 0.0))
            v = jnp.where(north | south, fix, v)
            put(step, pick(1, jnp.where(item < 5, v, 0.0)) + pick(0, jnp.where(item >= 5, v, 0.0)))

        @pl.when((me >= 10) & (me < 20))
        def _():
            v = whole(step)
            item = jnp.where(lane_y < 10, lane_y, (lane_y + turn - 10) % 10)
            put(step, pick(3, jnp.where(item < 5, v, 0.0)) + pick(2, jnp.where(item >= 5, v, 0.0)))

        @pl.when(is_z)
        def _():
            j = me - 20
            a = pick(jnp.where(j < 5, 5, 4), whole(step))
            on_x = (j == 1) | (j == 2) | (j == 6) | (j == 7)
            plus = (j == 1) | (j == 3) | (j == 7) | (j == 9)
            axial = (j == 0) | (j == 5)
            where = jnp.where(plus, 15, 0)
            hit = jnp.where(on_x, lane_x, lane_y) == jnp.where(axial, -1, where)
            side = jnp.where(on_x, 0, 2) + jnp.where(plus, 1, 0)
            put(step, jnp.where(hit, pick(side, a), a))

        @pl.when(me < 30)
        def _():
            def body(d, carry):
                peer = lax.rem(me + d, NB)
                remote(
                    ob.at[step, peer], rb.at[step, rows_of(me)], bsend.at[step], brecv.at[step], peer, layer
                ).start()
                return carry

            lax.fori_loop(1, NB, body, 0)
            rb[step, rows_of(me), :] = ob[step, me]

    def receive_b(step):
        @pl.when(me < 30)
        def _():
            wait_bytes(rb.at[step, pl.ds(0, 29 * 16)], brecv.at[step])

        @pl.when(me >= 30)
        def _():
            wait_bytes(rb.at[step, pl.ds(0, 30 * 16)], brecv.at[step])

    collide_all(0)
    pack_z(0)
    pack_x(0)
    pack_y(0)
    pl.semaphore_wait(barrier, (NB - 1) + 2 + 10)
    send_z(0)
    send_ten(0, 0)
    send_ten(0, 10)

    for copy in tables:
        copy.wait()
    nbf = jnp.concatenate([nbv[d] for d in range(6)] + [jnp.zeros((2, 256), jnp.int32)], axis=0).astype(f32)
    cols[...] = jnp.transpose(nbf)
    blank = jnp.zeros((48, 128), f32)
    for step in range(2):
        for first in (5, 13, 21, 29):
            rb[step, first * 16:first * 16 + 48, :] = blank

    @pl.loop(0, 256, step=32)
    def _(t):
        rows = pl.ds(pl.multiple_of(t, 32), 32)
        column = lax.broadcasted_iota(jnp.int32, (32, 256), 1).astype(f32)
        table = cols[rows, :]
        for d in range(6):
            pm[d, rows, :] = jnp.where(table[:, d:d + 1] == column, 1.0, 0.0).astype(jnp.bfloat16)

    shift_all()
    middle(0)
    receive_b(0)
    insert_all(0)

    collide_all(1)
    pack_z(1)
    send_z(1)
    pack_x(1)
    send_ten(1, 0)
    pack_y(1)
    send_ten(1, 10)

    zero = jnp.zeros((16, 128), f32)
    lane128 = lax.broadcasted_iota(jnp.int32, (1, 128), 1)

    def tile(t):
        return sens[t // 2, :, (t % 2) * 128:(t % 2) * 128 + 128] if 0 <= t < 16 else zero

    for t in range(17):
        before, here, after = tile(t - 1), tile(t), tile(t + 1)
        shifted[0, t] = jnp.where(lane128 < 32, pltpu.roll(before, 32, 1), pltpu.roll(here, 32, 1))
        shifted[1, t] = here
        shifted[2, t] = jnp.where(lane128 < 96, pltpu.roll(here, 96, 1), pltpu.roll(after, 96, 1))
        shifted[3, t] = jnp.where(lane128 < 64, pltpu.roll(here, 64, 1), pltpu.roll(after, 64, 1))

    def cut(j, pairs):
        s, t = pairs % 4, pairs // 4
        ss[j, :, :128] = shifted[s, t]
        ss[j, :, 128:] = shifted[s, t + 1]
        return pairs + oms[0, j]

    lax.fori_loop(0, NB, cut, jnp.int32(0))

    def send_rows(d, carry):
        peer = lax.rem(me + d, NB)
        remote(ss.at[peer], rs.at[me], ssend, srecv, peer, layer).start()
        return carry

    lax.fori_loop(1, NB, send_rows, 0)
    rs[me] = ss[me]

    shift_all()
    middle(1)

    wait_bytes(rs.at[pl.ds(0, NB - 1)], srecv)
    first = 2 * lax.fori_loop(0, NB, lambda i, acc: acc + jnp.where(i < me, oms[0, i], 0), jnp.int32(0))
    own_rows = 2 * oms[0, me]
    kf = (first + 14) // 16 - 1
    split = 16 * (kf + 1) - (first - 2)
    ka, kb = jnp.maximum(kf, 0), jnp.minimum(kf + 1, 7)

    def find(a, carry):
        ta, tb = carry
        ta = jnp.where(bxs[0, a * 8 + ka] == 0, a * 8 + ka, ta)
        tb = jnp.where(bxs[0, a * 8 + kb] == 0, a * 8 + kb, tb)
        return ta, tb

    start = lax.fori_loop(0, NB, find, (jnp.int32(0), jnp.int32(0)))
    group = lane128 // 16

    def arrange(cg, carry):
        ta, tb = carry
        parts = []
        for _ in range(8):
            parts.append(jnp.where(lane_y < split, rs[ta // 8], rs[tb // 8]))
            ta = jnp.maximum(nbx[0, ta], 0)
            tb = jnp.maximum(nbx[0, tb], 0)
        for r in range(16):
            h = r // 8
            acc = None
            for c in range(8):
                a = parts[c][:, h * 128:h * 128 + 128]
                s = ((c - r % 8) * 16) % 128
                if s:
                    a = pltpu.roll(a, s, 1)
                acc = a if acc is None else jnp.where(group == c, a, acc)
            fld[cg, r] = acc
        return ta, tb

    lax.fori_loop(0, 4, arrange, start)

    lane512 = lax.broadcasted_iota(jnp.int32, (1, 512), 1)
    third = 1.0 / 3.0

    def taps(a, b, c, d, e):
        return third * (a + e) + (2.0 * third) * (b + d) + c

    for r in range(12):
        row = lambda q: jnp.concatenate([fld[cg, q] for cg in range(4)], axis=1)
        v = taps(row(r), row(r + 1), row(r + 2), row(r + 3), row(r + 4))
        m2 = jnp.where(lane512 >= 2, pltpu.roll(v, 2, 1), 0.0)
        m1 = jnp.where(lane512 >= 1, pltpu.roll(v, 1, 1), 0.0)
        p1 = jnp.where(lane512 < 511, pltpu.roll(v, 511, 1), 0.0)
        p2 = jnp.where(lane512 < 510, pltpu.roll(v, 510, 1), 0.0)
        v = taps(m2, m1, v, p1, p2)
        flt[r] = v
        hs[0, 2 * r:2 * r + 2, :] = v[0:2, :]
        hs[1, 2 * r:2 * r + 2, :] = v[14:16, :]

    to_down = remote(hs.at[0], hr.at[1], hsend.at[0], hrecv.at[1], me, down)
    to_up = remote(hs.at[1], hr.at[0], hsend.at[1], hrecv.at[0], me, up)
    to_down.start()
    to_up.start()

    receive_b(1)
    insert_all(1)
    to_down.wait_send()
    to_up.wait_send()
    to_up.wait_recv()
    to_down.wait_recv()
    below = jnp.where(layer > 0, 1.0, 0.0)
    above = jnp.where(layer < NZ - 1, 1.0, 0.0)
    for r in range(12):
        v = jnp.concatenate(
            [hr[0, 2 * r:2 * r + 2, :] * below, flt[r], hr[1, 2 * r:2 * r + 2, :] * above], axis=0
        )
        v = taps(v[0:16], v[1:17], v[2:18], v[3:19], v[4:20])
        smo[0, 0, r] = jnp.where(own_rows > r, v, 0.0)

    for step in range(2):
        wait_bytes(sa.at[step, pl.ds(0, 10 * 16)], zsend.at[step])

        @pl.when(me < 20)
        def _():
            wait_bytes(sa.at[step, pl.ds(0, 19 * 16)], asend.at[step])

        @pl.when(me >= 20)
        def _():
            wait_bytes(sa.at[step, pl.ds(0, 20 * 16)], asend.at[step])

        @pl.when(me < 30)
        def _():
            wait_bytes(ob.at[step, pl.ds(0, NB - 1)], bsend.at[step])

    wait_bytes(ss.at[pl.ds(0, NB - 1)], ssend)


def local(adjoint, velocity, porosity, block_x, neighbours, owner_map):
    f32 = jnp.float32
    vmem = pl.BlockSpec(memory_space=pltpu.VMEM)
    hbm = pl.BlockSpec(memory_space=pltpu.HBM)
    dma = pltpu.SemaphoreType.DMA
    return pl.pallas_call(
        kernel,
        out_shape=(
            jax.ShapeDtypeStruct((1, 8, 19, 16, 256), f32),
            jax.ShapeDtypeStruct((1, 1, 12, 16, 512), f32),
        ),
        in_specs=[hbm] * 6,
        out_specs=(vmem, vmem),
        scratch_shapes=[
            pltpu.VMEM((8, 3, 16, 256), f32),
            pltpu.VMEM((8, 16, 256), f32),
            pltpu.VMEM((6, 1, 256), jnp.int32),
            pltpu.SMEM((1, 256), jnp.int32),
            pltpu.SMEM((1, 256), jnp.int32),
            pltpu.SMEM((1, NB), jnp.int32),
            pltpu.VMEM((256, 8), f32),
            pltpu.VMEM((8, 19, 16, 256), f32),
            pltpu.VMEM((8, 16, 256), f32),
            pltpu.VMEM((2, 42 * 16, 128), f32),
            pltpu.VMEM((2, NB, 16, 128), f32),
            pltpu.VMEM((2, NB, 16, 128), f32),
            pltpu.VMEM((2, 42 * 16, 128), f32),
            pltpu.VMEM((6, 256, 256), jnp.bfloat16),
            pltpu.VMEM((4, 17, 16, 128), f32),
            pltpu.VMEM((NB, 16, 256), f32),
            pltpu.VMEM((NB, 16, 256), f32),
            pltpu.VMEM((4, 16, 16, 128), f32),
            pltpu.VMEM((12, 16, 512), f32),
            pltpu.VMEM((2, 24, 512), f32),
            pltpu.VMEM((2, 24, 512), f32),
            dma((3, 8)), dma((4,)),
            dma((2,)), dma((2,)), dma((2,)),
            dma((2,)), dma((2,)),
            dma, dma,
            dma((2,)), dma((2,)),
        ],
        compiler_params=pltpu.CompilerParams(
            collective_id=0, has_side_effects=True, vmem_limit_bytes=48 * 1024 * 1024
        ),
    )(*(
        pltpu.with_memory_space_constraint(array, pltpu.HBM)
        for array in (
            adjoint, velocity, porosity, jnp.transpose(neighbours, (2, 0, 1)), block_x, owner_map.reshape(1, NB)
        )
    ))


def solution(mesh):
    placed = (
        P("gz", "blk", None, None, None),
        P("gz", "blk", None, None, None),
        P("gz", "blk", None, None),
        P("gz", None),
        P("gz", None, None),
        P(),
    )
    return jax.shard_map(
        local,
        mesh=mesh,
        in_specs=placed,
        out_specs=(P("gz", "blk", None, None, None), P("gz", "blk", None, None, None)),
        check_vma=False,
    )
```

```python
import functools

import jax
import jax.numpy as jnp
import numpy as np
from jax import lax
from jax.experimental import pallas as pl
from jax.experimental.pallas import tpu as pltpu
from jax.sharding import PartitionSpec as P

VEL = [
    (0, 0, 0),
    (1, 0, 0), (-1, 0, 0), (0, 1, 0), (0, -1, 0), (0, 0, 1), (0, 0, -1),
    (1, 1, 0), (-1, -1, 0), (1, -1, 0), (-1, 1, 0),
    (1, 0, 1), (-1, 0, -1), (1, 0, -1), (-1, 0, 1),
    (0, 1, 1), (0, -1, -1), (0, 1, -1), (0, -1, 1),
]
XPOPS = [1, 7, 9, 11, 13, 2, 8, 10, 12, 14]
YPOPS = [3, 7, 10, 15, 17, 4, 8, 9, 16, 18]
ZPOPS = [5, 11, 14, 15, 18, 6, 12, 13, 16, 17]
NB = 32
NZ = 4
MESH = pl.DeviceIdType.MESH


def collide(f, u, por):
    def total(parts):
        acc = parts[0]
        for part in parts[1:]:
            acc = acc + part
        return acc

    ux, uy, uz = u
    plus = lambda a, b: f[a] + f[b]
    minus = lambda a, b: f[a] - f[b]
    ax, ay, az = plus(1, 2), plus(3, 4), plus(5, 6)
    bx, by, bz = minus(1, 2), minus(3, 4), minus(5, 6)
    s78, s9a = plus(7, 8), plus(9, 10)
    d78, d9a = minus(7, 8), minus(9, 10)
    sbc, sde = plus(11, 12), plus(13, 14)
    dbc, dde = minus(11, 12), minus(13, 14)
    sfg, shi = plus(15, 16), plus(17, 18)
    dfg, dhi = minus(15, 16), minus(17, 18)
    dx = (d78 + d9a) + (dbc + dde)
    dy = (d78 - d9a) + (dfg + dhi)
    dz = (dbc - dde) + (dfg - dhi)
    momx, momy, momz = bx + dx, by + dy, bz + dz
    w1, w2 = 1.0 / 18.0, 1.0 / 36.0
    gx = w1 * bx + w2 * dx
    gy = w1 * by + w2 * dy
    gz = w1 * bz + w2 * dz
    xy, xz, yz = s78 + s9a, sbc + sde, sfg + shi
    qxx = w1 * ax + w2 * (xy + xz)
    qyy = w1 * ay + w2 * (xy + yz)
    qzz = w1 * az + w2 * (xz + yz)
    qxy = w2 * (s78 - s9a)
    qxz = w2 * (sbc - sde)
    qyz = w2 * (sfg - shi)
    weight = (1.0 / 3.0) * f[0] + w1 * (ax + ay + az) + w2 * (xy + xz + yz)
    qux = qxx * ux + qxy * uy + qxz * uz
    quy = qxy * ux + qyy * uy + qyz * uz
    quz = qxz * ux + qyz * uy + qzz * uz
    uu = ux * ux + uy * uy + uz * uz
    ug = ux * gx + uy * gy + uz * gz
    uqu = ux * qux + uy * quy + uz * quz
    um = ux * momx + uy * momy + uz * momz
    scalar = weight * (1.0 - 1.5 * uu) + 3.0 * ug + 4.5 * uqu
    uv = 3.0 * ug + 9.0 * uqu - 3.0 * uu * weight
    drag = 0.3 * por
    base = 1.25 * (scalar - uv) + drag * um
    ex = 1.25 * (3.0 * gx + 9.0 * qux - 3.0 * ux * weight) - drag * momx
    ey = 1.25 * (3.0 * gy + 9.0 * quy - 3.0 * uy * weight) - drag * momy
    ez = 1.25 * (3.0 * gz + 9.0 * quz - 3.0 * uz * weight) - drag * momz
    e = (ex, ey, ez)
    post = []
    for i, c in enumerate(VEL):
        acc = base - 0.25 * f[i]
        for axis in range(3):
            if c[axis] == 1:
                acc = acc + e[axis]
            elif c[axis] == -1:
                acc = acc - e[axis]
        post.append(acc)
    return post, um


MOVES = [
    (5, 0, 10, 10, 15), (5, 1, 4, 10, 13), (6, 1, 14, 14, 15), (6, 2, 8, 10, 15),
    (6, 3, 2, 10, 11), (7, 3, 12, 12, 15), (7, 4, 6, 10, 15),
]


HALVES = (slice(0, 128), slice(128, 256))


def spread(v, shift, axis):
    shift = shift % v.shape[axis]
    return pltpu.roll(v, shift, axis) if shift else v


def lanes128():
    lane = lax.broadcasted_iota(jnp.int32, (1, 128), 1)
    return lane % 16, lane // 16


def fold_x(rec, depth8):
    lx, _ = lanes128()
    out = []
    for v in rec:
        turned = {n: pltpu.roll(v, 16 - n, 0) for n in (3, 4, 5)}
        for z, q, s, low, high in MOVES:
            v = jnp.where((depth8 == q) & (lx >= low) & (lx <= high), spread(turned[z - q], s, 1), v)
        out.append(v)
    return out


def unfold_x(rec, depth8):
    lx, _ = lanes128()
    out = []
    for v in rec:
        turned = {n: pltpu.roll(v, n, 0) for n in (3, 4, 5)}
        for z, q, s, low, high in MOVES:
            v = jnp.where((depth8 == z) & (lx >= low - s) & (lx <= high - s), spread(turned[z - q], -s, 1), v)
        out.append(v)
    return out


def fold_y(rec, depth8):
    _, ly = lanes128()
    turned = [{n: pltpu.roll(v, 16 - n, 0) for n in (3, 4, 5)} for v in rec]
    low_half, v = rec
    for z, q, s, low, high in MOVES:
        for h in range(2):
            first, last = max(low - s, 8 * h) + s, min(high - s, 8 * h + 7) + s
            if first <= last:
                here = (depth8 == q) & (ly >= first - 8) & (ly <= last - 8)
                v = jnp.where(here, spread(turned[h][z - q], s * 16, 1), v)
    return [low_half, v]


def unfold_y(rec, depth8):
    _, ly = lanes128()
    turned = {n: pltpu.roll(rec[1], n, 0) for n in (3, 4, 5)}
    out = list(rec)
    for z, q, s, low, high in MOVES:
        moved = spread(turned[z - q], -s * 16, 1)
        for h in range(2):
            first, last = max(low - s, 8 * h), min(high - s, 8 * h + 7)
            if first <= last:
                here = (depth8 == z) & (ly >= first - 8 * h) & (ly <= last - 8 * h)
                out[h] = jnp.where(here, moved, out[h])
    return out


def put_faces(i, a, rx, ry):
    cx, cy, _ = VEL[i]
    lx, ly = lanes128()
    a = list(a)
    if cy:
        j = YPOPS.index(i)
        h, group = (1, 7) if cy == 1 else (0, 0)
        a[h] = jnp.where(ly == group, spread(ry[j // 8], (group - j % 8) * 16, 1), a[h])
    if cx:
        j = XPOPS.index(i)
        xt = 15 if cx == 1 else 0
        for h in range(2):
            a[h] = jnp.where(lx == xt, spread(rx[h], xt - j, 1), a[h])
    return a


def taps(a, b, c, d, e):
    third = 1.0 / 3.0
    return third * (a + e) + (2.0 * third) * (b + d) + c


def finish(inner, flt, halo, out, smo, slab, sem):
    copies = [pltpu.make_async_copy(inner.at[0, k], out.at[0, k], sem.at[k]) for k in range(8)]
    for copy in copies:
        copy.start()
    for r in range(12):
        v = jnp.concatenate([halo[0, 2 * r:2 * r + 2, :], flt[r], halo[1, 2 * r:2 * r + 2, :]], axis=0)
        slab[r] = taps(v[0:16], v[1:17], v[2:18], v[3:19], v[4:20])
    copies.append(pltpu.make_async_copy(slab, smo.at[0, 0], sem.at[8]))
    copies[-1].start()
    for copy in copies:
        copy.wait()


def kernel(
    adj, vel, por, nbt, bx, om, out, flt, halo_out,
    velv, porv, nbv, nbx, bxs, oms, cols,
    post, sens, sa, ra, ob, rb, pm, shifted, ss, rs, fld, hs, hr,
    lsem, tsem, asend, arecv, zsend, bsend, brecv, ssend, srecv, hsend, hrecv,
):
    me = lax.axis_index("blk")
    layer = lax.axis_index("gz")
    up, down = lax.rem(layer + 1, NZ), lax.rem(layer + NZ - 1, NZ)
    f32 = jnp.float32

    barrier = pltpu.get_barrier_semaphore()

    def signal(blk, gz):
        pl.semaphore_signal(barrier, inc=1, device_id={"blk": blk, "gz": gz}, device_id_type=MESH)

    def hello(d, carry):
        signal(lax.rem(me + d, NB), layer)
        return carry

    def hello_up(d, carry):
        signal(d, up)
        return carry

    def hello_down(d, carry):
        signal(d, down)
        return carry

    is_z = (me >= 20) & (me < 30)

    @pl.when((me >= 20) & (me < 25))
    def _():
        lax.fori_loop(0, NB, hello_up, 0)

    @pl.when((me >= 25) & (me < 30))
    def _():
        lax.fori_loop(0, NB, hello_down, 0)

    lax.fori_loop(1, NB, hello, 0)
    signal(me, up)
    signal(me, down)

    def loads(k):
        return (
            pltpu.make_async_copy(adj.at[0, k], out.at[0, k], lsem.at[0, k]),
            pltpu.make_async_copy(vel.at[0, k], velv.at[k], lsem.at[1, k]),
            pltpu.make_async_copy(por.at[0, k], porv.at[k], lsem.at[2, k]),
        )

    def load(k, carry):
        for copy in loads(k):
            copy.start()
        return carry

    lax.fori_loop(0, 8, load, 0)
    tables = (
        pltpu.make_async_copy(nbt, nbv, tsem.at[0]),
        pltpu.make_async_copy(nbt.at[1], nbx, tsem.at[1]),
        pltpu.make_async_copy(bx, bxs, tsem.at[2]),
        pltpu.make_async_copy(om, oms, tsem.at[3]),
    )
    for copy in tables:
        copy.start()

    lane = lax.broadcasted_iota(jnp.int32, (1, 256), 1)
    lane_x, lane_y = lane % 16, lane // 16
    depth = lax.broadcasted_iota(jnp.int32, (16, 1), 0)
    depth8 = depth % 8

    def collide_all(step):
        def body(k, carry):
            if step == 0:
                for copy in loads(k):
                    copy.wait()
            for half in range(2):
                rows = pl.ds(half * 8, 8)
                f = [out[0, k, i, rows, :] for i in range(19)]
                u = [velv[k, c, rows, :] for c in range(3)]
                new, um = collide(f, u, porv[k, rows, :])
                for i in range(19):
                    post[k, i, rows, :] = new[i]
                if step == 0:
                    sens[k, rows, :] = um
                else:
                    sens[k, rows, :] = sens[k, rows, :] + um
            return carry

        lax.fori_loop(0, 8, body, 0)

    def pack_x(step):
        lx, _ = lanes128()
        def body(k, carry):
            rec = [jnp.zeros((16, 128), f32)] * 2
            for j, i in enumerate(XPOPS):
                cx, cy, cz = VEL[i]
                x0 = 0 if cx == 1 else 15
                if cy:
                    a = spread(post[k, i], j - x0 - 16 * cy, 1)
                    a = [a[:, h] for h in HALVES]
                else:
                    a = [spread(spread(post[k, i, :, h], -cz, 0), j - x0, 1) for h in HALVES]
                rec = [jnp.where(lx == j, new, old) for new, old in zip(a, rec)]
            rec = fold_x(rec, depth8)
            for h in range(2):
                sa[step, pl.ds(k + 8 * h, 16, stride=16), :] = rec[h]
            return carry

        lax.fori_loop(0, 8, body, 0, unroll=True)

    def pack_y(step):
        _, ly = lanes128()
        def body(k, carry):
            rec = [jnp.zeros((16, 128), f32)] * 2
            for j, i in enumerate(YPOPS):
                cx, cy, cz = VEL[i]
                h, group = (0, 0) if cy == 1 else (1, 7)
                a = spread(spread(post[k, i, :, HALVES[h]], -cz, 0), (j % 8 - group) * 16 - cx, 1)
                rec[j // 8] = jnp.where(ly == j % 8, a, rec[j // 8])
            rec = fold_y(rec, depth8)
            for h in range(2):
                sa[step, pl.ds(256 + k + 8 * h, 16, stride=16), :] = rec[h]
            return carry

        lax.fori_loop(0, 8, body, 0, unroll=True)

    def pack_z(step):
        for j, i in enumerate(ZPOPS):
            cx, cy, cz = VEL[i]
            z0 = 0 if cz == 1 else 15
            a = jnp.concatenate([post[k, i, z0:z0 + 1, :] for k in range(8)], axis=0)
            if cx == 1:
                a = jnp.where(lane_x == 15, pltpu.roll(a, 15, 1), pltpu.roll(a, 255, 1))
            elif cx == -1:
                a = jnp.where(lane_x == 0, pltpu.roll(a, 241, 1), pltpu.roll(a, 1, 1))
            elif cy:
                a = pltpu.roll(a, (-16 * cy) % 256, 1)
            base = (32 + j) * 16
            sa[step, base:base + 8, :] = a[:, :128]
            sa[step, base + 8:base + 16, :] = a[:, 128:]

    def shift_all():
        def body(k, carry):
            for i, (cx, cy, cz) in enumerate(VEL):
                a = post[k, i]
                s = (-(16 * cy + cx)) % 256
                if s:
                    a = pltpu.roll(a, s, 1)
                if cz:
                    a = pltpu.roll(a, (-cz) % 16, 0)
                out[0, k, i] = a
            return carry

        lax.fori_loop(0, 8, body, 0)

    def insert_all(step):
        def body(k, carry):
            part = lambda first: [rb[step, pl.ds(first + k + 8 * h, 16, stride=16), :] for h in range(2)]
            rx, ry = unfold_x(part(0), depth8), unfold_y(part(256), depth8)
            for i, (cx, cy, cz) in enumerate(VEL):
                if cx or cy:
                    a = put_faces(i, [out[0, k, i, :, h] for h in HALVES], rx, ry)
                    for h in range(2):
                        if cx or h == (1 if cy == 1 else 0):
                            out[0, k, i, :, HALVES[h]] = a[h]
                if cz:
                    zt = 15 if cz == 1 else 0
                    first = (32 + ZPOPS.index(i)) * 16 + k
                    for h in range(2):
                        out[0, k, i, zt:zt + 1, HALVES[h]] = rb[step, pl.ds(first + 8 * h, 1), :]
            return carry

        lax.fori_loop(0, 8, body, 0, unroll=True)

    def remote(src, dst, send, recv, blk, gz):
        return pltpu.make_async_remote_copy(
            src_ref=src, dst_ref=dst, send_sem=send, recv_sem=recv,
            device_id={"blk": blk, "gz": gz}, device_id_type=MESH,
        )

    def far_first():
        hops = lambda o: min(o[0], 4 - o[0]) + min(o[1], 4 - o[1])
        others = [(z, y, c) for z in range(4) for y in range(4) for c in range(2)][1:]
        for z, y, c in sorted(others, key=lambda o: -hops(o)):
            yield (me // 8 + z) % 4 * 8 + (me // 2 + y) % 4 * 2 + (me + c) % 2

    def wait_bytes(ref, sem):
        pltpu.make_async_copy(ref, ref, sem).wait()

    def row_of(p):
        return jnp.where(p < 20, p // 5 * 8 + p % 5, p + 12) * 16

    def rows_of(p):
        return pl.ds(pl.multiple_of(row_of(p), 16), 16)

    def send_z(step):
        def body(j, carry):
            rows = pl.ds(pl.multiple_of((32 + j) * 16, 16), 16)
            dest = jnp.where(j < 5, down, up)
            remote(sa.at[step, rows], ra.at[step, me], zsend.at[step], arecv.at[step], 20 + j, dest).start()
            return carry

        lax.fori_loop(0, 10, body, 0)

    def send_ten(step, first):
        def body(d, carry):
            peer = first + lax.rem(me + d, 10)
            remote(
                sa.at[step, rows_of(peer)], ra.at[step, me], asend.at[step], arecv.at[step], peer, layer
            ).start()
            return carry

        mine = (me >= first) & (me < first + 10)

        @pl.when(mine)
        def _():
            ra[step, me] = sa[step, rows_of(me), :]
            lax.fori_loop(1, 10, body, 0)

        @pl.when(jnp.logical_not(mine))
        def _():
            lax.fori_loop(0, 10, body, 0)

    def split3(v):
        hi = v.astype(jnp.bfloat16)
        rest = v - hi.astype(f32)
        mid = rest.astype(jnp.bfloat16)
        low = (rest - mid.astype(f32)).astype(jnp.bfloat16)
        return hi, mid, low

    def pick(d, v):
        p = pm[d]
        hi, mid, low = split3(v)
        dot = lambda part: jnp.dot(p, part, preferred_element_type=f32)
        return (dot(hi) + dot(mid)) + dot(low)

    def whole(step):
        return jnp.concatenate(
            [ra[step, :, 0:8, :].reshape(256, 128), ra[step, :, 8:16, :].reshape(256, 128)], axis=1
        )

    def put(step, v):
        ob[step, :, 0:8, :] = v[:, :128].reshape(NB, 8, 128)
        ob[step, :, 8:16, :] = v[:, 128:].reshape(NB, 8, 128)

    def middle(step):
        turn = me % 5 * 6

        @pl.when(me < 20)
        def _():
            wait_bytes(ra.at[step, pl.ds(0, NB - 1)], arecv.at[step])

        @pl.when(is_z)
        def _():
            wait_bytes(ra.at[step], arecv.at[step])

        @pl.when(me < 10)
        def _():
            v = whole(step)
            item = jnp.where(lane_x < 10, lane_x, (lane_x + turn - 10) % 10)
            north = (lane_y == 15) & ((item == 1) | (item == 7))
            south = (lane_y == 0) & ((item == 2) | (item == 6))
            fix = jnp.concatenate([pick(2, v[:, :128]), pick(3, v[:, 128:])], axis=1)
            v = jnp.where(north | south, fix, v)
            put(step, pick(1, jnp.where(item < 5, v, 0.0)) + pick(0, jnp.where(item >= 5, v, 0.0)))

        @pl.when((me >= 10) & (me < 20))
        def _():
            v = whole(step)
            item = jnp.where(lane_y < 10, lane_y, (lane_y + turn - 10) % 10)
            put(step, pick(3, jnp.where(item < 5, v, 0.0)) + pick(2, jnp.where(item >= 5, v, 0.0)))

        @pl.when(is_z)
        def _():
            j = me - 20
            a = pick(jnp.where(j < 5, 5, 4), whole(step))
            on_x = (j == 1) | (j == 2) | (j == 6) | (j == 7)
            plus = (j == 1) | (j == 3) | (j == 7) | (j == 9)
            axial = (j == 0) | (j == 5)
            where = jnp.where(plus, 15, 0)
            hit = jnp.where(on_x, lane_x, lane_y) == jnp.where(axial, -1, where)
            side = jnp.where(on_x, 0, 2) + jnp.where(plus, 1, 0)
            put(step, jnp.where(hit, pick(side, a), a))

        @pl.when(me < 30)
        def _():
            for peer in far_first():
                remote(
                    ob.at[step, peer], rb.at[step, rows_of(me)], bsend.at[step], brecv.at[step], peer, layer
                ).start()
            rb[step, rows_of(me), :] = ob[step, me]

    def receive_b(step):
        @pl.when(me < 30)
        def _():
            wait_bytes(rb.at[step, pl.ds(0, 29 * 16)], brecv.at[step])

        @pl.when(me >= 30)
        def _():
            wait_bytes(rb.at[step, pl.ds(0, 30 * 16)], brecv.at[step])

    collide_all(0)
    pack_z(0)
    pack_x(0)
    pack_y(0)
    pl.semaphore_wait(barrier, (NB - 1) + 2 + 10)
    send_z(0)
    send_ten(0, 0)
    send_ten(0, 10)

    for copy in tables:
        copy.wait()
    nbf = jnp.concatenate([nbv[d] for d in range(6)] + [jnp.zeros((2, 256), jnp.int32)], axis=0).astype(f32)
    cols[...] = jnp.transpose(nbf)
    blank = jnp.zeros((48, 128), f32)
    for step in range(2):
        for first in (5, 13, 21, 29):
            rb[step, first * 16:first * 16 + 48, :] = blank

    @pl.loop(0, 256, step=32)
    def _(t):
        rows = pl.ds(pl.multiple_of(t, 32), 32)
        column = lax.broadcasted_iota(jnp.int32, (32, 256), 1).astype(f32)
        table = cols[rows, :]
        for d in range(6):
            pm[d, rows, :] = jnp.where(table[:, d:d + 1] == column, 1.0, 0.0).astype(jnp.bfloat16)

    shift_all()
    middle(0)
    receive_b(0)
    insert_all(0)

    collide_all(1)
    pack_z(1)
    send_z(1)
    pack_x(1)
    send_ten(1, 0)
    pack_y(1)
    send_ten(1, 10)

    zero = jnp.zeros((16, 128), f32)
    lane128 = lax.broadcasted_iota(jnp.int32, (1, 128), 1)

    def tile(t):
        return sens[t // 2, :, (t % 2) * 128:(t % 2) * 128 + 128] if 0 <= t < 16 else zero

    for t in range(17):
        before, here, after = tile(t - 1), tile(t), tile(t + 1)
        shifted[0, t] = jnp.where(lane128 < 32, pltpu.roll(before, 32, 1), pltpu.roll(here, 32, 1))
        shifted[1, t] = here
        shifted[2, t] = jnp.where(lane128 < 96, pltpu.roll(here, 96, 1), pltpu.roll(after, 96, 1))
        shifted[3, t] = jnp.where(lane128 < 64, pltpu.roll(here, 64, 1), pltpu.roll(after, 64, 1))

    def cut(j, pairs):
        s, t = pairs % 4, pairs // 4
        ss[j, :, :128] = shifted[s, t]
        ss[j, :, 128:] = shifted[s, t + 1]
        return pairs + oms[0, j]

    lax.fori_loop(0, NB, cut, jnp.int32(0), unroll=True)

    for peer in far_first():
        remote(ss.at[peer], rs.at[me], ssend, srecv, peer, layer).start()
    rs[me] = ss[me]

    shift_all()
    middle(1)

    wait_bytes(rs.at[pl.ds(0, NB - 1)], srecv)
    first = 2 * lax.fori_loop(0, NB, lambda i, acc: acc + jnp.where(i < me, oms[0, i], 0), jnp.int32(0))
    own_rows = 2 * oms[0, me]
    kf = (first + 14) // 16 - 1
    split = 16 * (kf + 1) - (first - 2)
    ka, kb = jnp.maximum(kf, 0), jnp.minimum(kf + 1, 7)

    def find(a, carry):
        ta, tb = carry
        ta = jnp.where(bxs[0, a * 8 + ka] == 0, a * 8 + ka, ta)
        tb = jnp.where(bxs[0, a * 8 + kb] == 0, a * 8 + kb, tb)
        return ta, tb

    start = lax.fori_loop(0, NB, find, (jnp.int32(0), jnp.int32(0)))
    group = lane128 // 16

    def arrange(cg, carry):
        ta, tb = carry
        parts = []
        for _ in range(8):
            parts.append(jnp.where(lane_y < split, rs[ta // 8], rs[tb // 8]))
            ta = jnp.maximum(nbx[0, ta], 0)
            tb = jnp.maximum(nbx[0, tb], 0)
        for r in range(16):
            h = r // 8
            acc = None
            for c in range(8):
                a = parts[c][:, h * 128:h * 128 + 128]
                s = ((c - r % 8) * 16) % 128
                if s:
                    a = pltpu.roll(a, s, 1)
                acc = a if acc is None else jnp.where(group == c, a, acc)
            fld[cg, r] = acc
        return ta, tb

    lax.fori_loop(0, 4, arrange, start)

    lane512 = lax.broadcasted_iota(jnp.int32, (1, 512), 1)
    for r in range(12):
        row = lambda q: jnp.concatenate([fld[cg, q] for cg in range(4)], axis=1)
        v = taps(row(r), row(r + 1), row(r + 2), row(r + 3), row(r + 4))
        m2 = jnp.where(lane512 >= 2, pltpu.roll(v, 2, 1), 0.0)
        m1 = jnp.where(lane512 >= 1, pltpu.roll(v, 1, 1), 0.0)
        p1 = jnp.where(lane512 < 511, pltpu.roll(v, 511, 1), 0.0)
        p2 = jnp.where(lane512 < 510, pltpu.roll(v, 510, 1), 0.0)
        v = jnp.where(own_rows > r, taps(m2, m1, v, p1, p2), 0.0)
        flt[r] = v
        hs[0, 2 * r:2 * r + 2, :] = v[0:2, :]
        hs[1, 2 * r:2 * r + 2, :] = v[14:16, :]

    to_down = remote(hs.at[0], hr.at[1], hsend.at[0], hrecv.at[1], me, down)
    to_up = remote(hs.at[1], hr.at[0], hsend.at[1], hrecv.at[0], me, up)
    to_down.start()
    to_up.start()

    receive_b(1)
    insert_all(1)

    to_down.wait_send()
    to_up.wait_send()
    to_up.wait_recv()
    to_down.wait_recv()
    halo_out[0] = hr[0] * jnp.where(layer > 0, 1.0, 0.0)
    halo_out[1] = hr[1] * jnp.where(layer < NZ - 1, 1.0, 0.0)

    for step in range(2):
        wait_bytes(sa.at[step, pl.ds(0, 10 * 16)], zsend.at[step])

        @pl.when(me < 20)
        def _():
            wait_bytes(sa.at[step, pl.ds(0, 19 * 16)], asend.at[step])

        @pl.when(me >= 20)
        def _():
            wait_bytes(sa.at[step, pl.ds(0, 20 * 16)], asend.at[step])

        @pl.when(me < 30)
        def _():
            wait_bytes(ob.at[step, pl.ds(0, NB - 1)], bsend.at[step])

    wait_bytes(ss.at[pl.ds(0, NB - 1)], ssend)


def local(adjoint, velocity, porosity, block_x, neighbours, owner_map):
    f32 = jnp.float32
    vmem = pl.BlockSpec(memory_space=pltpu.VMEM)
    hbm = pl.BlockSpec(memory_space=pltpu.HBM)
    dma = pltpu.SemaphoreType.DMA
    inner, flt, halo = pl.pallas_call(
        kernel,
        out_shape=(
            jax.ShapeDtypeStruct((1, 8, 19, 16, 256), f32),
            jax.ShapeDtypeStruct((12, 16, 512), f32),
            jax.ShapeDtypeStruct((2, 24, 512), f32),
        ),
        in_specs=[hbm] * 6,
        out_specs=(vmem,) * 3,
        scratch_shapes=[
            pltpu.VMEM((8, 3, 16, 256), f32),
            pltpu.VMEM((8, 16, 256), f32),
            pltpu.VMEM((6, 1, 256), jnp.int32),
            pltpu.SMEM((1, 256), jnp.int32),
            pltpu.SMEM((1, 256), jnp.int32),
            pltpu.SMEM((1, NB), jnp.int32),
            pltpu.VMEM((256, 8), f32),
            pltpu.VMEM((8, 19, 16, 256), f32),
            pltpu.VMEM((8, 16, 256), f32),
            pltpu.VMEM((2, 42 * 16, 128), f32),
            pltpu.VMEM((2, NB, 16, 128), f32),
            pltpu.VMEM((2, NB, 16, 128), f32),
            pltpu.VMEM((2, 42 * 16, 128), f32),
            pltpu.VMEM((6, 256, 256), jnp.bfloat16),
            pltpu.VMEM((4, 17, 16, 128), f32),
            pltpu.VMEM((NB, 16, 256), f32),
            pltpu.VMEM((NB, 16, 256), f32),
            pltpu.VMEM((4, 16, 16, 128), f32),
            pltpu.VMEM((2, 24, 512), f32),
            pltpu.VMEM((2, 24, 512), f32),
            dma((3, 8)), dma((4,)),
            dma((2,)), dma((2,)), dma((2,)),
            dma((2,)), dma((2,)),
            dma, dma,
            dma((2,)), dma((2,)),
        ],
        compiler_params=pltpu.CompilerParams(
            collective_id=0, has_side_effects=True, vmem_limit_bytes=48 * 1024 * 1024
        ),
    )(*(
        pltpu.with_memory_space_constraint(array, pltpu.HBM)
        for array in (
            adjoint, velocity, porosity, jnp.transpose(neighbours, (2, 0, 1)), block_x, owner_map.reshape(1, NB)
        )
    ))
    return pl.pallas_call(
        finish,
        out_shape=(
            jax.ShapeDtypeStruct((1, 8, 19, 16, 256), f32),
            jax.ShapeDtypeStruct((1, 1, 12, 16, 512), f32),
        ),
        in_specs=[vmem] * 3,
        out_specs=(hbm, hbm),
        scratch_shapes=[
            pltpu.VMEM((12, 16, 512), f32),
            dma((9,)),
        ],
        compiler_params=pltpu.CompilerParams(vmem_limit_bytes=32 * 1024 * 1024),
    )(inner, flt, halo)


def solution(mesh):
    placed = (
        P("gz", "blk", None, None, None),
        P("gz", "blk", None, None, None),
        P("gz", "blk", None, None),
        P("gz", None),
        P("gz", None, None),
        P(),
    )
    return jax.shard_map(
        local,
        mesh=mesh,
        in_specs=placed,
        out_specs=(P("gz", "blk", None, None, None), P("gz", "blk", None, None, None)),
        check_vma=False,
    )
```

```python
import functools

import jax
import jax.numpy as jnp
import numpy as np
from jax import lax
from jax.experimental import pallas as pl
from jax.experimental.pallas import tpu as pltpu
from jax.sharding import PartitionSpec as P

VEL = [
    (0, 0, 0),
    (1, 0, 0), (-1, 0, 0), (0, 1, 0), (0, -1, 0), (0, 0, 1), (0, 0, -1),
    (1, 1, 0), (-1, -1, 0), (1, -1, 0), (-1, 1, 0),
    (1, 0, 1), (-1, 0, -1), (1, 0, -1), (-1, 0, 1),
    (0, 1, 1), (0, -1, -1), (0, 1, -1), (0, -1, 1),
]
XPOPS = [1, 7, 9, 11, 13, 2, 8, 10, 12, 14]
YPOPS = [3, 7, 10, 15, 17, 4, 8, 9, 16, 18]
ZPOPS = [5, 11, 14, 15, 18, 6, 12, 13, 16, 17]
NB = 32
NZ = 4
MESH = pl.DeviceIdType.MESH


def collide(f, u, por):
    def total(parts):
        acc = parts[0]
        for part in parts[1:]:
            acc = acc + part
        return acc

    ux, uy, uz = u
    plus = lambda a, b: f[a] + f[b]
    minus = lambda a, b: f[a] - f[b]
    ax, ay, az = plus(1, 2), plus(3, 4), plus(5, 6)
    bx, by, bz = minus(1, 2), minus(3, 4), minus(5, 6)
    s78, s9a = plus(7, 8), plus(9, 10)
    d78, d9a = minus(7, 8), minus(9, 10)
    sbc, sde = plus(11, 12), plus(13, 14)
    dbc, dde = minus(11, 12), minus(13, 14)
    sfg, shi = plus(15, 16), plus(17, 18)
    dfg, dhi = minus(15, 16), minus(17, 18)
    dx = (d78 + d9a) + (dbc + dde)
    dy = (d78 - d9a) + (dfg + dhi)
    dz = (dbc - dde) + (dfg - dhi)
    momx, momy, momz = bx + dx, by + dy, bz + dz
    w1, w2 = 1.0 / 18.0, 1.0 / 36.0
    gx = w1 * bx + w2 * dx
    gy = w1 * by + w2 * dy
    gz = w1 * bz + w2 * dz
    xy, xz, yz = s78 + s9a, sbc + sde, sfg + shi
    qxx = w1 * ax + w2 * (xy + xz)
    qyy = w1 * ay + w2 * (xy + yz)
    qzz = w1 * az + w2 * (xz + yz)
    qxy = w2 * (s78 - s9a)
    qxz = w2 * (sbc - sde)
    qyz = w2 * (sfg - shi)
    weight = (1.0 / 3.0) * f[0] + w1 * (ax + ay + az) + w2 * (xy + xz + yz)
    qux = qxx * ux + qxy * uy + qxz * uz
    quy = qxy * ux + qyy * uy + qyz * uz
    quz = qxz * ux + qyz * uy + qzz * uz
    uu = ux * ux + uy * uy + uz * uz
    ug = ux * gx + uy * gy + uz * gz
    uqu = ux * qux + uy * quy + uz * quz
    um = ux * momx + uy * momy + uz * momz
    scalar = weight * (1.0 - 1.5 * uu) + 3.0 * ug + 4.5 * uqu
    uv = 3.0 * ug + 9.0 * uqu - 3.0 * uu * weight
    drag = 0.3 * por
    base = 1.25 * (scalar - uv) + drag * um
    ex = 1.25 * (3.0 * gx + 9.0 * qux - 3.0 * ux * weight) - drag * momx
    ey = 1.25 * (3.0 * gy + 9.0 * quy - 3.0 * uy * weight) - drag * momy
    ez = 1.25 * (3.0 * gz + 9.0 * quz - 3.0 * uz * weight) - drag * momz
    e = (ex, ey, ez)
    post = []
    for i, c in enumerate(VEL):
        acc = base - 0.25 * f[i]
        for axis in range(3):
            if c[axis] == 1:
                acc = acc + e[axis]
            elif c[axis] == -1:
                acc = acc - e[axis]
        post.append(acc)
    return post, um


MOVES = [
    (5, 0, 10, 10, 15), (5, 1, 4, 10, 13), (6, 1, 14, 14, 15), (6, 2, 8, 10, 15),
    (6, 3, 2, 10, 11), (7, 3, 12, 12, 15), (7, 4, 6, 10, 15),
]


HALVES = (slice(0, 128), slice(128, 256))


def spread(v, shift, axis):
    shift = shift % v.shape[axis]
    return pltpu.roll(v, shift, axis) if shift else v


def lanes128():
    lane = lax.broadcasted_iota(jnp.int32, (1, 128), 1)
    return lane % 16, lane // 16


def fold_x(rec, depth8):
    lx, _ = lanes128()
    out = []
    for v in rec:
        turned = {n: pltpu.roll(v, 16 - n, 0) for n in (3, 4, 5)}
        for z, q, s, low, high in MOVES:
            v = jnp.where((depth8 == q) & (lx >= low) & (lx <= high), spread(turned[z - q], s, 1), v)
        out.append(v)
    return out


def unfold_x(rec, depth8):
    lx, _ = lanes128()
    out = []
    for v in rec:
        turned = {n: pltpu.roll(v, n, 0) for n in (3, 4, 5)}
        for z, q, s, low, high in MOVES:
            v = jnp.where((depth8 == z) & (lx >= low - s) & (lx <= high - s), spread(turned[z - q], -s, 1), v)
        out.append(v)
    return out


def fold_y(rec, depth8):
    _, ly = lanes128()
    turned = [{n: pltpu.roll(v, 16 - n, 0) for n in (3, 4, 5)} for v in rec]
    low_half, v = rec
    for z, q, s, low, high in MOVES:
        for h in range(2):
            first, last = max(low - s, 8 * h) + s, min(high - s, 8 * h + 7) + s
            if first <= last:
                here = (depth8 == q) & (ly >= first - 8) & (ly <= last - 8)
                v = jnp.where(here, spread(turned[h][z - q], s * 16, 1), v)
    return [low_half, v]


def unfold_y(rec, depth8):
    _, ly = lanes128()
    turned = {n: pltpu.roll(rec[1], n, 0) for n in (3, 4, 5)}
    out = list(rec)
    for z, q, s, low, high in MOVES:
        moved = spread(turned[z - q], -s * 16, 1)
        for h in range(2):
            first, last = max(low - s, 8 * h), min(high - s, 8 * h + 7)
            if first <= last:
                here = (depth8 == z) & (ly >= first - 8 * h) & (ly <= last - 8 * h)
                out[h] = jnp.where(here, moved, out[h])
    return out


def put_faces(i, a, rx, ry):
    cx, cy, _ = VEL[i]
    lx, ly = lanes128()
    a = list(a)
    if cy:
        j = YPOPS.index(i)
        h, group = (1, 7) if cy == 1 else (0, 0)
        a[h] = jnp.where(ly == group, spread(ry[j // 8], (group - j % 8) * 16, 1), a[h])
    if cx:
        j = XPOPS.index(i)
        xt = 15 if cx == 1 else 0
        for h in range(2):
            a[h] = jnp.where(lx == xt, spread(rx[h], xt - j, 1), a[h])
    return a


def taps(a, b, c, d, e):
    third = 1.0 / 3.0
    return third * (a + e) + (2.0 * third) * (b + d) + c


def finish(inner, flt, halo, out, smo, slab, sem):
    copies = [pltpu.make_async_copy(inner.at[0, k], out.at[0, k], sem.at[k]) for k in range(8)]
    for copy in copies:
        copy.start()
    for r in range(12):
        v = jnp.concatenate([halo[0, 2 * r:2 * r + 2, :], flt[r], halo[1, 2 * r:2 * r + 2, :]], axis=0)
        slab[r] = taps(v[0:16], v[1:17], v[2:18], v[3:19], v[4:20])
    copies.append(pltpu.make_async_copy(slab, smo.at[0, 0], sem.at[8]))
    copies[-1].start()
    for copy in copies:
        copy.wait()


def kernel(
    adj, vel, por, nbt, bx, om, out, flt, halo_out,
    velv, porv, nbv, nbx, bxs, oms, cols,
    post, sens, sa, ra, ob, rb, pm, shifted, ss, rs, fld, hs, hr,
    lsem, tsem, asend, arecv, zsend, bsend, brecv, ssend, srecv, hsend, hrecv,
):
    me = lax.axis_index("blk")
    layer = lax.axis_index("gz")
    up, down = lax.rem(layer + 1, NZ), lax.rem(layer + NZ - 1, NZ)
    f32 = jnp.float32

    barrier = pltpu.get_barrier_semaphore()

    def signal(blk, gz):
        pl.semaphore_signal(barrier, inc=1, device_id={"blk": blk, "gz": gz}, device_id_type=MESH)

    def hello(d, carry):
        signal(lax.rem(me + d, NB), layer)
        return carry

    def hello_up(d, carry):
        signal(d, up)
        return carry

    def hello_down(d, carry):
        signal(d, down)
        return carry

    is_z = (me >= 20) & (me < 30)

    @pl.when((me >= 20) & (me < 25))
    def _():
        lax.fori_loop(0, NB, hello_up, 0)

    @pl.when((me >= 25) & (me < 30))
    def _():
        lax.fori_loop(0, NB, hello_down, 0)

    lax.fori_loop(1, NB, hello, 0)
    signal(me, up)
    signal(me, down)

    def loads(k):
        return (
            pltpu.make_async_copy(adj.at[0, k], out.at[0, k], lsem.at[0, k]),
            pltpu.make_async_copy(vel.at[0, k], velv.at[k], lsem.at[1, k]),
            pltpu.make_async_copy(por.at[0, k], porv.at[k], lsem.at[2, k]),
        )

    def load(k, carry):
        for copy in loads(k):
            copy.start()
        return carry

    lax.fori_loop(0, 8, load, 0)
    tables = (
        pltpu.make_async_copy(nbt, nbv, tsem.at[0]),
        pltpu.make_async_copy(nbt.at[1], nbx, tsem.at[1]),
        pltpu.make_async_copy(bx, bxs, tsem.at[2]),
        pltpu.make_async_copy(om, oms, tsem.at[3]),
    )
    for copy in tables:
        copy.start()

    lane = lax.broadcasted_iota(jnp.int32, (1, 256), 1)
    lane_x, lane_y = lane % 16, lane // 16
    depth = lax.broadcasted_iota(jnp.int32, (16, 1), 0)
    depth8 = depth % 8

    def collide_all(step):
        def body(k, carry):
            if step == 0:
                for copy in loads(k):
                    copy.wait()
            for half in range(2):
                rows = pl.ds(half * 8, 8)
                f = [out[0, k, i, rows, :] for i in range(19)]
                u = [velv[k, c, rows, :] for c in range(3)]
                new, um = collide(f, u, porv[k, rows, :])
                for i in range(19):
                    post[k, i, rows, :] = new[i]
                if step == 0:
                    sens[k, rows, :] = um
                else:
                    sens[k, rows, :] = sens[k, rows, :] + um
            return carry

        lax.fori_loop(0, 8, body, 0)

    def pack_x(step):
        lx, _ = lanes128()
        def body(k, carry):
            rec = [jnp.zeros((16, 128), f32)] * 2
            for j, i in enumerate(XPOPS):
                cx, cy, cz = VEL[i]
                x0 = 0 if cx == 1 else 15
                if cy:
                    a = spread(post[k, i], j - x0 - 16 * cy, 1)
                    a = [a[:, h] for h in HALVES]
                else:
                    a = [spread(spread(post[k, i, :, h], -cz, 0), j - x0, 1) for h in HALVES]
                rec = [jnp.where(lx == j, new, old) for new, old in zip(a, rec)]
            rec = fold_x(rec, depth8)
            for h in range(2):
                sa[step, pl.ds(k + 8 * h, 16, stride=16), :] = rec[h]
            return carry

        lax.fori_loop(0, 8, body, 0, unroll=True)

    def pack_y(step):
        _, ly = lanes128()
        def body(k, carry):
            rec = [jnp.zeros((16, 128), f32)] * 2
            for j, i in enumerate(YPOPS):
                cx, cy, cz = VEL[i]
                h, group = (0, 0) if cy == 1 else (1, 7)
                a = spread(spread(post[k, i, :, HALVES[h]], -cz, 0), (j % 8 - group) * 16 - cx, 1)
                rec[j // 8] = jnp.where(ly == j % 8, a, rec[j // 8])
            rec = fold_y(rec, depth8)
            for h in range(2):
                sa[step, pl.ds(256 + k + 8 * h, 16, stride=16), :] = rec[h]
            return carry

        lax.fori_loop(0, 8, body, 0, unroll=True)

    def pack_z(step):
        for j, i in enumerate(ZPOPS):
            cx, cy, cz = VEL[i]
            z0 = 0 if cz == 1 else 15
            a = jnp.concatenate([post[k, i, z0:z0 + 1, :] for k in range(8)], axis=0)
            if cx == 1:
                a = jnp.where(lane_x == 15, pltpu.roll(a, 15, 1), pltpu.roll(a, 255, 1))
            elif cx == -1:
                a = jnp.where(lane_x == 0, pltpu.roll(a, 241, 1), pltpu.roll(a, 1, 1))
            elif cy:
                a = pltpu.roll(a, (-16 * cy) % 256, 1)
            base = (32 + j) * 16
            sa[step, base:base + 8, :] = a[:, :128]
            sa[step, base + 8:base + 16, :] = a[:, 128:]

    def shift_all():
        def body(k, carry):
            for i, (cx, cy, cz) in enumerate(VEL):
                a = post[k, i]
                s = (-(16 * cy + cx)) % 256
                if s:
                    a = pltpu.roll(a, s, 1)
                if cz:
                    a = pltpu.roll(a, (-cz) % 16, 0)
                out[0, k, i] = a
            return carry

        lax.fori_loop(0, 8, body, 0)

    def collide_faces(step):
        lx, ly = lanes128()

        def block(k):
            part = lambda first: [rb[step, pl.ds(first + k + 8 * h, 16, stride=16), :] for h in range(2)]
            rx, ry = unfold_x(part(0), depth8), unfold_y(part(256), depth8)
            for h in range(2):
                f = []
                for i, (cx, cy, cz) in enumerate(VEL):
                    a = out[0, k, i, :, HALVES[h]]
                    if cy and h == (1 if cy == 1 else 0):
                        j = YPOPS.index(i)
                        group = 7 if cy == 1 else 0
                        a = jnp.where(ly == group, spread(ry[j // 8], (group - j % 8) * 16, 1), a)
                    if cx:
                        xt = 15 if cx == 1 else 0
                        a = jnp.where(lx == xt, spread(rx[h], xt - XPOPS.index(i), 1), a)
                    if cz:
                        first = (32 + ZPOPS.index(i)) * 16 + k + 8 * h
                        a = jnp.where(depth == (15 if cz == 1 else 0), rb[step, pl.ds(first, 1), :], a)
                    f.append(a)
                u = [velv[k, c, :, HALVES[h]] for c in range(3)]
                new, um = collide(f, u, porv[k, :, HALVES[h]])
                for i in range(19):
                    post[k, i, :, HALVES[h]] = new[i]
                sens[k, :, HALVES[h]] = sens[k, :, HALVES[h]] + um

        def body(t, carry):
            for n in range(4):
                block(4 * t + n)
            return carry

        lax.fori_loop(0, 2, body, 0)

    def insert_all(step):
        def body(k, carry):
            part = lambda first: [rb[step, pl.ds(first + k + 8 * h, 16, stride=16), :] for h in range(2)]
            rx, ry = unfold_x(part(0), depth8), unfold_y(part(256), depth8)
            for i, (cx, cy, cz) in enumerate(VEL):
                if cx or cy:
                    a = put_faces(i, [out[0, k, i, :, h] for h in HALVES], rx, ry)
                    for h in range(2):
                        if cx or h == (1 if cy == 1 else 0):
                            out[0, k, i, :, HALVES[h]] = a[h]
                if cz:
                    zt = 15 if cz == 1 else 0
                    first = (32 + ZPOPS.index(i)) * 16 + k
                    for h in range(2):
                        out[0, k, i, zt:zt + 1, HALVES[h]] = rb[step, pl.ds(first + 8 * h, 1), :]
            return carry

        lax.fori_loop(0, 8, body, 0, unroll=True)

    def remote(src, dst, send, recv, blk, gz):
        return pltpu.make_async_remote_copy(
            src_ref=src, dst_ref=dst, send_sem=send, recv_sem=recv,
            device_id={"blk": blk, "gz": gz}, device_id_type=MESH,
        )

    def far_first():
        hops = lambda o: min(o[0], 4 - o[0]) + min(o[1], 4 - o[1])
        others = [(z, y, c) for z in range(4) for y in range(4) for c in range(2)][1:]
        for z, y, c in sorted(others, key=lambda o: -hops(o)):
            yield (me // 8 + z) % 4 * 8 + (me // 2 + y) % 4 * 2 + (me + c) % 2

    def wait_bytes(ref, sem):
        pltpu.make_async_copy(ref, ref, sem).wait()

    def row_of(p):
        return jnp.where(p < 20, p // 5 * 8 + p % 5, p + 12) * 16

    def rows_of(p):
        return pl.ds(pl.multiple_of(row_of(p), 16), 16)

    def send_z(step):
        def body(j, carry):
            rows = pl.ds(pl.multiple_of((32 + j) * 16, 16), 16)
            dest = jnp.where(j < 5, down, up)
            remote(sa.at[step, rows], ra.at[step, me], zsend.at[step], arecv.at[step], 20 + j, dest).start()
            return carry

        lax.fori_loop(0, 10, body, 0)

    def send_ten(step, first):
        def body(d, carry):
            peer = first + lax.rem(me + d, 10)
            remote(
                sa.at[step, rows_of(peer)], ra.at[step, me], asend.at[step], arecv.at[step], peer, layer
            ).start()
            return carry

        mine = (me >= first) & (me < first + 10)

        @pl.when(mine)
        def _():
            ra[step, me] = sa[step, rows_of(me), :]
            lax.fori_loop(1, 10, body, 0)

        @pl.when(jnp.logical_not(mine))
        def _():
            lax.fori_loop(0, 10, body, 0)

    def split3(v):
        hi = v.astype(jnp.bfloat16)
        rest = v - hi.astype(f32)
        mid = rest.astype(jnp.bfloat16)
        low = (rest - mid.astype(f32)).astype(jnp.bfloat16)
        return hi, mid, low

    def pick(d, v):
        p = pm[d]
        hi, mid, low = split3(v)
        dot = lambda part: jnp.dot(p, part, preferred_element_type=f32)
        return (dot(hi) + dot(mid)) + dot(low)

    def whole(step):
        return jnp.concatenate(
            [ra[step, :, 0:8, :].reshape(256, 128), ra[step, :, 8:16, :].reshape(256, 128)], axis=1
        )

    def put(step, v):
        ob[step, :, 0:8, :] = v[:, :128].reshape(NB, 8, 128)
        ob[step, :, 8:16, :] = v[:, 128:].reshape(NB, 8, 128)

    def middle(step):
        turn = me % 5 * 6

        @pl.when(me < 20)
        def _():
            wait_bytes(ra.at[step, pl.ds(0, NB - 1)], arecv.at[step])

        @pl.when(is_z)
        def _():
            wait_bytes(ra.at[step], arecv.at[step])

        @pl.when(me < 10)
        def _():
            v = whole(step)
            item = jnp.where(lane_x < 10, lane_x, (lane_x + turn - 10) % 10)
            north = (lane_y == 15) & ((item == 1) | (item == 7))
            south = (lane_y == 0) & ((item == 2) | (item == 6))
            fix = jnp.concatenate([pick(2, v[:, :128]), pick(3, v[:, 128:])], axis=1)
            v = jnp.where(north | south, fix, v)
            put(step, pick(1, jnp.where(item < 5, v, 0.0)) + pick(0, jnp.where(item >= 5, v, 0.0)))

        @pl.when((me >= 10) & (me < 20))
        def _():
            v = whole(step)
            item = jnp.where(lane_y < 10, lane_y, (lane_y + turn - 10) % 10)
            put(step, pick(3, jnp.where(item < 5, v, 0.0)) + pick(2, jnp.where(item >= 5, v, 0.0)))

        @pl.when(is_z)
        def _():
            j = me - 20
            a = pick(jnp.where(j < 5, 5, 4), whole(step))
            on_x = (j == 1) | (j == 2) | (j == 6) | (j == 7)
            plus = (j == 1) | (j == 3) | (j == 7) | (j == 9)
            axial = (j == 0) | (j == 5)
            where = jnp.where(plus, 15, 0)
            hit = jnp.where(on_x, lane_x, lane_y) == jnp.where(axial, -1, where)
            side = jnp.where(on_x, 0, 2) + jnp.where(plus, 1, 0)
            put(step, jnp.where(hit, pick(side, a), a))

        @pl.when(me < 30)
        def _():
            for peer in far_first():
                remote(
                    ob.at[step, peer], rb.at[step, rows_of(me)], bsend.at[step], brecv.at[step], peer, layer
                ).start()
            rb[step, rows_of(me), :] = ob[step, me]

    def receive_b(step):
        @pl.when(me < 30)
        def _():
            wait_bytes(rb.at[step, pl.ds(0, 29 * 16)], brecv.at[step])

        @pl.when(me >= 30)
        def _():
            wait_bytes(rb.at[step, pl.ds(0, 30 * 16)], brecv.at[step])

    collide_all(0)
    pack_z(0)
    pack_x(0)
    pack_y(0)
    pl.semaphore_wait(barrier, (NB - 1) + 2 + 10)
    send_z(0)
    send_ten(0, 0)
    send_ten(0, 10)

    for copy in tables:
        copy.wait()
    nbf = jnp.concatenate([nbv[d] for d in range(6)] + [jnp.zeros((2, 256), jnp.int32)], axis=0).astype(f32)
    cols[...] = jnp.transpose(nbf)
    blank = jnp.zeros((48, 128), f32)
    for step in range(2):
        for first in (5, 13, 21, 29):
            rb[step, first * 16:first * 16 + 48, :] = blank

    @pl.loop(0, 256, step=32)
    def _(t):
        rows = pl.ds(pl.multiple_of(t, 32), 32)
        column = lax.broadcasted_iota(jnp.int32, (32, 256), 1).astype(f32)
        table = cols[rows, :]
        for d in range(6):
            pm[d, rows, :] = jnp.where(table[:, d:d + 1] == column, 1.0, 0.0).astype(jnp.bfloat16)

    shift_all()
    middle(0)
    receive_b(0)

    collide_faces(0)
    pack_z(1)
    send_z(1)
    pack_x(1)
    send_ten(1, 0)
    pack_y(1)
    send_ten(1, 10)

    zero = jnp.zeros((16, 128), f32)
    lane128 = lax.broadcasted_iota(jnp.int32, (1, 128), 1)

    def tile(t):
        return sens[t // 2, :, (t % 2) * 128:(t % 2) * 128 + 128] if 0 <= t < 16 else zero

    for t in range(17):
        before, here, after = tile(t - 1), tile(t), tile(t + 1)
        shifted[0, t] = jnp.where(lane128 < 32, pltpu.roll(before, 32, 1), pltpu.roll(here, 32, 1))
        shifted[1, t] = here
        shifted[2, t] = jnp.where(lane128 < 96, pltpu.roll(here, 96, 1), pltpu.roll(after, 96, 1))
        shifted[3, t] = jnp.where(lane128 < 64, pltpu.roll(here, 64, 1), pltpu.roll(after, 64, 1))

    def cut(j, pairs):
        s, t = pairs % 4, pairs // 4
        ss[j, :, :128] = shifted[s, t]
        ss[j, :, 128:] = shifted[s, t + 1]
        return pairs + oms[0, j]

    lax.fori_loop(0, NB, cut, jnp.int32(0), unroll=True)

    for half in range(2):
        rows = pl.ds(half * 8, 8)
        for peer in far_first():
            remote(ss.at[peer, rows], rs.at[me, rows], ssend, srecv, peer, layer).start()
    rs[me] = ss[me]

    shift_all()
    middle(1)

    wait_bytes(rs.at[pl.ds(0, NB - 1)], srecv)
    first = 2 * lax.fori_loop(0, NB, lambda i, acc: acc + jnp.where(i < me, oms[0, i], 0), jnp.int32(0))
    own_rows = 2 * oms[0, me]
    kf = (first + 14) // 16 - 1
    split = 16 * (kf + 1) - (first - 2)
    ka, kb = jnp.maximum(kf, 0), jnp.minimum(kf + 1, 7)

    def find(a, carry):
        ta, tb = carry
        ta = jnp.where(bxs[0, a * 8 + ka] == 0, a * 8 + ka, ta)
        tb = jnp.where(bxs[0, a * 8 + kb] == 0, a * 8 + kb, tb)
        return ta, tb

    start = lax.fori_loop(0, NB, find, (jnp.int32(0), jnp.int32(0)))
    group = lane128 // 16

    def arrange(cg, carry):
        ta, tb = carry
        parts = []
        for _ in range(8):
            parts.append(jnp.where(lane_y < split, rs[ta // 8], rs[tb // 8]))
            ta = jnp.maximum(nbx[0, ta], 0)
            tb = jnp.maximum(nbx[0, tb], 0)
        for r in range(16):
            h = r // 8
            acc = None
            for c in range(8):
                a = parts[c][:, h * 128:h * 128 + 128]
                s = ((c - r % 8) * 16) % 128
                if s:
                    a = pltpu.roll(a, s, 1)
                acc = a if acc is None else jnp.where(group == c, a, acc)
            fld[cg, r] = acc
            lanes = pl.ds(pl.multiple_of(cg * 128, 128), 128)
            hs[0, 2 * r:2 * r + 2, lanes] = acc[0:2, :]
            hs[1, 2 * r:2 * r + 2, lanes] = acc[14:16, :]
        return ta, tb

    lax.fori_loop(0, 4, arrange, start)

    to_down = remote(hs.at[0], hr.at[1], hsend.at[0], hrecv.at[1], me, down)
    to_up = remote(hs.at[1], hr.at[0], hsend.at[1], hrecv.at[0], me, up)
    to_down.start()
    to_up.start()

    lane512 = lax.broadcasted_iota(jnp.int32, (1, 512), 1)
    def along_x(v):
        m2 = jnp.where(lane512 >= 2, pltpu.roll(v, 2, 1), 0.0)
        m1 = jnp.where(lane512 >= 1, pltpu.roll(v, 1, 1), 0.0)
        p1 = jnp.where(lane512 < 511, pltpu.roll(v, 511, 1), 0.0)
        p2 = jnp.where(lane512 < 510, pltpu.roll(v, 510, 1), 0.0)
        return taps(m2, m1, v, p1, p2)

    for r in range(12):
        row = lambda q: jnp.concatenate([fld[cg, q] for cg in range(4)], axis=1)
        v = taps(row(r), row(r + 1), row(r + 2), row(r + 3), row(r + 4))
        flt[r] = jnp.where(own_rows > r, along_x(v), 0.0)

    receive_b(1)
    insert_all(1)

    to_down.wait_send()
    to_up.wait_send()
    to_up.wait_recv()
    to_down.wait_recv()
    wanted = lax.broadcasted_iota(jnp.int32, (24, 1), 0) // 2 < own_rows
    for side, there in enumerate((layer > 0, layer < NZ - 1)):
        v = hr[side]
        v = along_x(taps(v[0:24], v[2:26], v[4:28], v[6:30], v[8:32]))
        halo_out[side] = jnp.where(wanted, v, 0.0) * jnp.where(there, 1.0, 0.0)

    for step in range(2):
        wait_bytes(sa.at[step, pl.ds(0, 10 * 16)], zsend.at[step])

        @pl.when(me < 20)
        def _():
            wait_bytes(sa.at[step, pl.ds(0, 19 * 16)], asend.at[step])

        @pl.when(me >= 20)
        def _():
            wait_bytes(sa.at[step, pl.ds(0, 20 * 16)], asend.at[step])

        @pl.when(me < 30)
        def _():
            wait_bytes(ob.at[step, pl.ds(0, NB - 1)], bsend.at[step])

    wait_bytes(ss.at[pl.ds(0, NB - 1)], ssend)


def local(adjoint, velocity, porosity, block_x, neighbours, owner_map):
    f32 = jnp.float32
    vmem = pl.BlockSpec(memory_space=pltpu.VMEM)
    hbm = pl.BlockSpec(memory_space=pltpu.HBM)
    dma = pltpu.SemaphoreType.DMA
    inner, flt, halo = pl.pallas_call(
        kernel,
        out_shape=(
            jax.ShapeDtypeStruct((1, 8, 19, 16, 256), f32),
            jax.ShapeDtypeStruct((12, 16, 512), f32),
            jax.ShapeDtypeStruct((2, 24, 512), f32),
        ),
        in_specs=[hbm] * 6,
        out_specs=(vmem,) * 3,
        scratch_shapes=[
            pltpu.VMEM((8, 3, 16, 256), f32),
            pltpu.VMEM((8, 16, 256), f32),
            pltpu.VMEM((6, 1, 256), jnp.int32),
            pltpu.SMEM((1, 256), jnp.int32),
            pltpu.SMEM((1, 256), jnp.int32),
            pltpu.SMEM((1, NB), jnp.int32),
            pltpu.VMEM((256, 8), f32),
            pltpu.VMEM((8, 19, 16, 256), f32),
            pltpu.VMEM((8, 16, 256), f32),
            pltpu.VMEM((2, 42 * 16, 128), f32),
            pltpu.VMEM((2, NB, 16, 128), f32),
            pltpu.VMEM((2, NB, 16, 128), f32),
            pltpu.VMEM((2, 42 * 16, 128), f32),
            pltpu.VMEM((6, 256, 256), jnp.bfloat16),
            pltpu.VMEM((4, 17, 16, 128), f32),
            pltpu.VMEM((NB, 16, 256), f32),
            pltpu.VMEM((NB, 16, 256), f32),
            pltpu.VMEM((4, 16, 16, 128), f32),
            pltpu.VMEM((2, 32, 512), f32),
            pltpu.VMEM((2, 32, 512), f32),
            dma((3, 8)), dma((4,)),
            dma((2,)), dma((2,)), dma((2,)),
            dma((2,)), dma((2,)),
            dma, dma,
            dma((2,)), dma((2,)),
        ],
        compiler_params=pltpu.CompilerParams(
            collective_id=0, has_side_effects=True, vmem_limit_bytes=48 * 1024 * 1024
        ),
    )(*(
        pltpu.with_memory_space_constraint(array, pltpu.HBM)
        for array in (
            adjoint, velocity, porosity, jnp.transpose(neighbours, (2, 0, 1)), block_x, owner_map.reshape(1, NB)
        )
    ))
    return pl.pallas_call(
        finish,
        out_shape=(
            jax.ShapeDtypeStruct((1, 8, 19, 16, 256), f32),
            jax.ShapeDtypeStruct((1, 1, 12, 16, 512), f32),
        ),
        in_specs=[vmem] * 3,
        out_specs=(hbm, hbm),
        scratch_shapes=[
            pltpu.VMEM((12, 16, 512), f32),
            dma((9,)),
        ],
        compiler_params=pltpu.CompilerParams(vmem_limit_bytes=32 * 1024 * 1024),
    )(inner, flt, halo)


def solution(mesh):
    placed = (
        P("gz", "blk", None, None, None),
        P("gz", "blk", None, None, None),
        P("gz", "blk", None, None),
        P("gz", None),
        P("gz", None, None),
        P(),
    )
    return jax.shard_map(
        local,
        mesh=mesh,
        in_specs=placed,
        out_specs=(P("gz", "blk", None, None, None), P("gz", "blk", None, None, None)),
        check_vma=False,
    )
```

```python
import functools

import jax
import jax.numpy as jnp
import numpy as np
from jax import lax
from jax.experimental import pallas as pl
from jax.experimental.pallas import tpu as pltpu
from jax.sharding import PartitionSpec as P

VEL = [
    (0, 0, 0),
    (1, 0, 0), (-1, 0, 0), (0, 1, 0), (0, -1, 0), (0, 0, 1), (0, 0, -1),
    (1, 1, 0), (-1, -1, 0), (1, -1, 0), (-1, 1, 0),
    (1, 0, 1), (-1, 0, -1), (1, 0, -1), (-1, 0, 1),
    (0, 1, 1), (0, -1, -1), (0, 1, -1), (0, -1, 1),
]
XPOPS = [1, 7, 9, 11, 13, 2, 8, 10, 12, 14]
YPOPS = [3, 7, 10, 15, 17, 4, 8, 9, 16, 18]
ZPOPS = [5, 11, 14, 15, 18, 6, 12, 13, 16, 17]
NB = 32
NZ = 4
MESH = pl.DeviceIdType.MESH


def collide(f, u, por):
    def total(parts):
        acc = parts[0]
        for part in parts[1:]:
            acc = acc + part
        return acc

    ux, uy, uz = u
    plus = lambda a, b: f[a] + f[b]
    minus = lambda a, b: f[a] - f[b]
    ax, ay, az = plus(1, 2), plus(3, 4), plus(5, 6)
    bx, by, bz = minus(1, 2), minus(3, 4), minus(5, 6)
    s78, s9a = plus(7, 8), plus(9, 10)
    d78, d9a = minus(7, 8), minus(9, 10)
    sbc, sde = plus(11, 12), plus(13, 14)
    dbc, dde = minus(11, 12), minus(13, 14)
    sfg, shi = plus(15, 16), plus(17, 18)
    dfg, dhi = minus(15, 16), minus(17, 18)
    dx = (d78 + d9a) + (dbc + dde)
    dy = (d78 - d9a) + (dfg + dhi)
    dz = (dbc - dde) + (dfg - dhi)
    momx, momy, momz = bx + dx, by + dy, bz + dz
    w1, w2 = 1.0 / 18.0, 1.0 / 36.0
    gx = w1 * bx + w2 * dx
    gy = w1 * by + w2 * dy
    gz = w1 * bz + w2 * dz
    xy, xz, yz = s78 + s9a, sbc + sde, sfg + shi
    qxx = w1 * ax + w2 * (xy + xz)
    qyy = w1 * ay + w2 * (xy + yz)
    qzz = w1 * az + w2 * (xz + yz)
    qxy = w2 * (s78 - s9a)
    qxz = w2 * (sbc - sde)
    qyz = w2 * (sfg - shi)
    weight = (1.0 / 3.0) * f[0] + w1 * (ax + ay + az) + w2 * (xy + xz + yz)
    qux = qxx * ux + qxy * uy + qxz * uz
    quy = qxy * ux + qyy * uy + qyz * uz
    quz = qxz * ux + qyz * uy + qzz * uz
    uu = ux * ux + uy * uy + uz * uz
    ug = ux * gx + uy * gy + uz * gz
    uqu = ux * qux + uy * quy + uz * quz
    um = ux * momx + uy * momy + uz * momz
    scalar = weight * (1.0 - 1.5 * uu) + 3.0 * ug + 4.5 * uqu
    uv = 3.0 * ug + 9.0 * uqu - 3.0 * uu * weight
    drag = 0.3 * por
    base = 1.25 * (scalar - uv) + drag * um
    ex = 1.25 * (3.0 * gx + 9.0 * qux - 3.0 * ux * weight) - drag * momx
    ey = 1.25 * (3.0 * gy + 9.0 * quy - 3.0 * uy * weight) - drag * momy
    ez = 1.25 * (3.0 * gz + 9.0 * quz - 3.0 * uz * weight) - drag * momz
    e = (ex, ey, ez)
    post = []
    for i, c in enumerate(VEL):
        acc = base - 0.25 * f[i]
        for axis in range(3):
            if c[axis] == 1:
                acc = acc + e[axis]
            elif c[axis] == -1:
                acc = acc - e[axis]
        post.append(acc)
    return post, um


MOVES = [
    (5, 0, 10, 10, 15), (5, 1, 4, 10, 13), (6, 1, 14, 14, 15), (6, 2, 8, 10, 15),
    (6, 3, 2, 10, 11), (7, 3, 12, 12, 15), (7, 4, 6, 10, 15),
]


HALVES = (slice(0, 128), slice(128, 256))


def spread(v, shift, axis):
    shift = shift % v.shape[axis]
    return pltpu.roll(v, shift, axis) if shift else v


def lanes128():
    lane = lax.broadcasted_iota(jnp.int32, (1, 128), 1)
    return lane % 16, lane // 16


def fold_x(rec, depth8):
    lx, _ = lanes128()
    out = []
    for v in rec:
        turned = {n: pltpu.roll(v, 16 - n, 0) for n in (3, 4, 5)}
        for z, q, s, low, high in MOVES:
            v = jnp.where((depth8 == q) & (lx >= low) & (lx <= high), spread(turned[z - q], s, 1), v)
        out.append(v)
    return out


def unfold_x(rec, depth8):
    lx, _ = lanes128()
    out = []
    for v in rec:
        turned = {n: pltpu.roll(v, n, 0) for n in (3, 4, 5)}
        for z, q, s, low, high in MOVES:
            v = jnp.where((depth8 == z) & (lx >= low - s) & (lx <= high - s), spread(turned[z - q], -s, 1), v)
        out.append(v)
    return out


def fold_y(rec, depth8):
    _, ly = lanes128()
    turned = [{n: pltpu.roll(v, 16 - n, 0) for n in (3, 4, 5)} for v in rec]
    low_half, v = rec
    for z, q, s, low, high in MOVES:
        for h in range(2):
            first, last = max(low - s, 8 * h) + s, min(high - s, 8 * h + 7) + s
            if first <= last:
                here = (depth8 == q) & (ly >= first - 8) & (ly <= last - 8)
                v = jnp.where(here, spread(turned[h][z - q], s * 16, 1), v)
    return [low_half, v]


def unfold_y(rec, depth8):
    _, ly = lanes128()
    turned = {n: pltpu.roll(rec[1], n, 0) for n in (3, 4, 5)}
    out = list(rec)
    for z, q, s, low, high in MOVES:
        moved = spread(turned[z - q], -s * 16, 1)
        for h in range(2):
            first, last = max(low - s, 8 * h), min(high - s, 8 * h + 7)
            if first <= last:
                here = (depth8 == z) & (ly >= first - 8 * h) & (ly <= last - 8 * h)
                out[h] = jnp.where(here, moved, out[h])
    return out


def put_faces(i, a, rx, ry):
    cx, cy, _ = VEL[i]
    lx, ly = lanes128()
    a = list(a)
    if cy:
        j = YPOPS.index(i)
        h, group = (1, 7) if cy == 1 else (0, 0)
        a[h] = jnp.where(ly == group, spread(ry[j // 8], (group - j % 8) * 16, 1), a[h])
    if cx:
        j = XPOPS.index(i)
        xt = 15 if cx == 1 else 0
        for h in range(2):
            a[h] = jnp.where(lx == xt, spread(rx[h], xt - j, 1), a[h])
    return a


def taps(a, b, c, d, e):
    third = 1.0 / 3.0
    return third * (a + e) + (2.0 * third) * (b + d) + c


def finish(inner, flt, halo, out, smo, slab, sem):
    copies = [pltpu.make_async_copy(inner.at[0, k], out.at[0, k], sem.at[k]) for k in range(8)]
    for copy in copies:
        copy.start()
    for r in range(12):
        v = jnp.concatenate([halo[0, 2 * r:2 * r + 2, :], flt[r], halo[1, 2 * r:2 * r + 2, :]], axis=0)
        slab[r] = taps(v[0:16], v[1:17], v[2:18], v[3:19], v[4:20])
    copies.append(pltpu.make_async_copy(slab, smo.at[0, 0], sem.at[8]))
    copies[-1].start()
    for copy in copies:
        copy.wait()


def kernel(
    adj, vel, por, nbt, bx, om, out, flt, halo_out,
    velv, porv, nbv, nbx, bxs, oms, cols,
    post, sens, sa, ra, ob, rb, pm, shifted, ss, rs, fld, hs, hr,
    lsem, tsem, asend, arecv, zsend, bsend, brecv, ssend, srecv, hsend, hrecv,
):
    me = lax.axis_index("blk")
    layer = lax.axis_index("gz")
    up, down = lax.rem(layer + 1, NZ), lax.rem(layer + NZ - 1, NZ)
    f32 = jnp.float32

    barrier = pltpu.get_barrier_semaphore()

    def signal(blk, gz):
        pl.semaphore_signal(barrier, inc=1, device_id={"blk": blk, "gz": gz}, device_id_type=MESH)

    def hello(d, carry):
        signal(lax.rem(me + d, NB), layer)
        return carry

    def hello_up(d, carry):
        signal(d, up)
        return carry

    def hello_down(d, carry):
        signal(d, down)
        return carry

    is_z = (me >= 20) & (me < 30)

    @pl.when((me >= 20) & (me < 25))
    def _():
        lax.fori_loop(0, NB, hello_up, 0)

    @pl.when((me >= 25) & (me < 30))
    def _():
        lax.fori_loop(0, NB, hello_down, 0)

    lax.fori_loop(1, NB, hello, 0)
    signal(me, up)
    signal(me, down)

    def loads(k):
        return (
            pltpu.make_async_copy(adj.at[0, k], out.at[0, k], lsem.at[0, k]),
            pltpu.make_async_copy(vel.at[0, k], velv.at[k], lsem.at[1, k]),
            pltpu.make_async_copy(por.at[0, k], porv.at[k], lsem.at[2, k]),
        )

    def load(k, carry):
        for copy in loads(k):
            copy.start()
        return carry

    lax.fori_loop(0, 8, load, 0)
    tables = (
        pltpu.make_async_copy(nbt, nbv, tsem.at[0]),
        pltpu.make_async_copy(nbt.at[1], nbx, tsem.at[1]),
        pltpu.make_async_copy(bx, bxs, tsem.at[2]),
        pltpu.make_async_copy(om, oms, tsem.at[3]),
    )
    for copy in tables:
        copy.start()

    lane = lax.broadcasted_iota(jnp.int32, (1, 256), 1)
    lane_x, lane_y = lane % 16, lane // 16
    depth = lax.broadcasted_iota(jnp.int32, (16, 1), 0)
    depth8 = depth % 8

    def collide_all(step):
        def body(k, carry):
            if step == 0:
                for copy in loads(k):
                    copy.wait()
            for half in range(2):
                rows = pl.ds(half * 8, 8)
                f = [out[0, k, i, rows, :] for i in range(19)]
                u = [velv[k, c, rows, :] for c in range(3)]
                new, um = collide(f, u, porv[k, rows, :])
                for i in range(19):
                    post[k, i, rows, :] = new[i]
                if step == 0:
                    sens[k, rows, :] = um
                else:
                    sens[k, rows, :] = sens[k, rows, :] + um
            return carry

        lax.fori_loop(0, 8, body, 0)

    def pack_x(step):
        lx, _ = lanes128()
        def body(k, carry):
            rec = [jnp.zeros((16, 128), f32)] * 2
            for j, i in enumerate(XPOPS):
                cx, cy, cz = VEL[i]
                x0 = 0 if cx == 1 else 15
                if cy:
                    a = spread(post[k, i], j - x0 - 16 * cy, 1)
                    a = [a[:, h] for h in HALVES]
                else:
                    a = [spread(spread(post[k, i, :, h], -cz, 0), j - x0, 1) for h in HALVES]
                rec = [jnp.where(lx == j, new, old) for new, old in zip(a, rec)]
            rec = fold_x(rec, depth8)
            for h in range(2):
                sa[step, pl.ds(k + 8 * h, 16, stride=16), :] = rec[h]
            return carry

        lax.fori_loop(0, 8, body, 0, unroll=True)

    def pack_y(step):
        _, ly = lanes128()
        def body(k, carry):
            rec = [jnp.zeros((16, 128), f32)] * 2
            for j, i in enumerate(YPOPS):
                cx, cy, cz = VEL[i]
                h, group = (0, 0) if cy == 1 else (1, 7)
                a = spread(spread(post[k, i, :, HALVES[h]], -cz, 0), (j % 8 - group) * 16 - cx, 1)
                rec[j // 8] = jnp.where(ly == j % 8, a, rec[j // 8])
            rec = fold_y(rec, depth8)
            for h in range(2):
                sa[step, pl.ds(256 + k + 8 * h, 16, stride=16), :] = rec[h]
            return carry

        lax.fori_loop(0, 8, body, 0, unroll=True)

    def pack_z(step):
        for j, i in enumerate(ZPOPS):
            cx, cy, cz = VEL[i]
            z0 = 0 if cz == 1 else 15
            a = jnp.concatenate([post[k, i, z0:z0 + 1, :] for k in range(8)], axis=0)
            if cx == 1:
                a = jnp.where(lane_x == 15, pltpu.roll(a, 15, 1), pltpu.roll(a, 255, 1))
            elif cx == -1:
                a = jnp.where(lane_x == 0, pltpu.roll(a, 241, 1), pltpu.roll(a, 1, 1))
            elif cy:
                a = pltpu.roll(a, (-16 * cy) % 256, 1)
            base = (32 + j) * 16
            sa[step, base:base + 8, :] = a[:, :128]
            sa[step, base + 8:base + 16, :] = a[:, 128:]

    def shift_all():
        def body(k, carry):
            for i, (cx, cy, cz) in enumerate(VEL):
                a = post[k, i]
                s = (-(16 * cy + cx)) % 256
                if s:
                    a = pltpu.roll(a, s, 1)
                if cz:
                    a = pltpu.roll(a, (-cz) % 16, 0)
                out[0, k, i] = a
            return carry

        lax.fori_loop(0, 8, body, 0)

    def collide_faces(step):
        lx, ly = lanes128()

        def block(k):
            part = lambda first: [rb[step, pl.ds(first + k + 8 * h, 16, stride=16), :] for h in range(2)]
            rx, ry = unfold_x(part(0), depth8), unfold_y(part(256), depth8)
            for h in range(2):
                f = []
                for i, (cx, cy, cz) in enumerate(VEL):
                    a = out[0, k, i, :, HALVES[h]]
                    if cy and h == (1 if cy == 1 else 0):
                        j = YPOPS.index(i)
                        group = 7 if cy == 1 else 0
                        a = jnp.where(ly == group, spread(ry[j // 8], (group - j % 8) * 16, 1), a)
                    if cx:
                        xt = 15 if cx == 1 else 0
                        a = jnp.where(lx == xt, spread(rx[h], xt - XPOPS.index(i), 1), a)
                    if cz:
                        first = (32 + ZPOPS.index(i)) * 16 + k + 8 * h
                        a = jnp.where(depth == (15 if cz == 1 else 0), rb[step, pl.ds(first, 1), :], a)
                    f.append(a)
                u = [velv[k, c, :, HALVES[h]] for c in range(3)]
                new, um = collide(f, u, porv[k, :, HALVES[h]])
                for i in range(19):
                    post[k, i, :, HALVES[h]] = new[i]
                sens[k, :, HALVES[h]] = sens[k, :, HALVES[h]] + um

        def body(t, carry):
            for n in range(8):
                block(8 * t + n)
            return carry

        lax.fori_loop(0, 1, body, 0)

    def insert_all(step):
        def body(k, carry):
            part = lambda first: [rb[step, pl.ds(first + k + 8 * h, 16, stride=16), :] for h in range(2)]
            rx, ry = unfold_x(part(0), depth8), unfold_y(part(256), depth8)
            for i, (cx, cy, cz) in enumerate(VEL):
                if cx or cy:
                    a = put_faces(i, [out[0, k, i, :, h] for h in HALVES], rx, ry)
                    for h in range(2):
                        if cx or h == (1 if cy == 1 else 0):
                            out[0, k, i, :, HALVES[h]] = a[h]
                if cz:
                    zt = 15 if cz == 1 else 0
                    first = (32 + ZPOPS.index(i)) * 16 + k
                    for h in range(2):
                        out[0, k, i, zt:zt + 1, HALVES[h]] = rb[step, pl.ds(first + 8 * h, 1), :]
            return carry

        lax.fori_loop(0, 8, body, 0, unroll=True)

    def remote(src, dst, send, recv, blk, gz):
        return pltpu.make_async_remote_copy(
            src_ref=src, dst_ref=dst, send_sem=send, recv_sem=recv,
            device_id={"blk": blk, "gz": gz}, device_id_type=MESH,
        )

    def far_first():
        hops = lambda o: min(o[0], 4 - o[0]) + min(o[1], 4 - o[1])
        others = [(z, y, c) for z in range(4) for y in range(4) for c in range(2)][1:]
        for z, y, c in sorted(others, key=lambda o: -hops(o)):
            yield (me // 8 + z) % 4 * 8 + (me // 2 + y) % 4 * 2 + (me + c) % 2

    def wait_bytes(ref, sem):
        pltpu.make_async_copy(ref, ref, sem).wait()

    def row_of(p):
        return jnp.where(p < 20, p // 5 * 8 + p % 5, p + 12) * 16

    def rows_of(p):
        return pl.ds(pl.multiple_of(row_of(p), 16), 16)

    def send_z(step):
        def body(j, carry):
            rows = pl.ds(pl.multiple_of((32 + j) * 16, 16), 16)
            dest = jnp.where(j < 5, down, up)
            remote(sa.at[step, rows], ra.at[step, me], zsend.at[step], arecv.at[step], 20 + j, dest).start()
            return carry

        lax.fori_loop(0, 10, body, 0)

    def send_ten(step, first):
        def body(d, carry):
            peer = first + lax.rem(me + d, 10)
            remote(
                sa.at[step, rows_of(peer)], ra.at[step, me], asend.at[step], arecv.at[step], peer, layer
            ).start()
            return carry

        mine = (me >= first) & (me < first + 10)

        @pl.when(mine)
        def _():
            ra[step, me] = sa[step, rows_of(me), :]
            lax.fori_loop(1, 10, body, 0)

        @pl.when(jnp.logical_not(mine))
        def _():
            lax.fori_loop(0, 10, body, 0)

    def split3(v):
        hi = v.astype(jnp.bfloat16)
        rest = v - hi.astype(f32)
        mid = rest.astype(jnp.bfloat16)
        low = (rest - mid.astype(f32)).astype(jnp.bfloat16)
        return hi, mid, low

    def pick(d, v):
        p = pm[d]
        hi, mid, low = split3(v)
        dot = lambda part: jnp.dot(p, part, preferred_element_type=f32)
        return (dot(hi) + dot(mid)) + dot(low)

    def whole(step):
        return jnp.concatenate(
            [ra[step, :, 0:8, :].reshape(256, 128), ra[step, :, 8:16, :].reshape(256, 128)], axis=1
        )

    def put(step, v):
        ob[step, :, 0:8, :] = v[:, :128].reshape(NB, 8, 128)
        ob[step, :, 8:16, :] = v[:, 128:].reshape(NB, 8, 128)

    def middle(step):
        turn = me % 5 * 6

        @pl.when(me < 20)
        def _():
            wait_bytes(ra.at[step, pl.ds(0, NB - 1)], arecv.at[step])

        @pl.when(is_z)
        def _():
            wait_bytes(ra.at[step], arecv.at[step])

        @pl.when(me < 10)
        def _():
            v = whole(step)
            item = jnp.where(lane_x < 10, lane_x, (lane_x + turn - 10) % 10)
            north = (lane_y == 15) & ((item == 1) | (item == 7))
            south = (lane_y == 0) & ((item == 2) | (item == 6))
            fix = jnp.concatenate([pick(2, v[:, :128]), pick(3, v[:, 128:])], axis=1)
            v = jnp.where(north | south, fix, v)
            put(step, pick(1, jnp.where(item < 5, v, 0.0)) + pick(0, jnp.where(item >= 5, v, 0.0)))

        @pl.when((me >= 10) & (me < 20))
        def _():
            v = whole(step)
            item = jnp.where(lane_y < 10, lane_y, (lane_y + turn - 10) % 10)
            put(step, pick(3, jnp.where(item < 5, v, 0.0)) + pick(2, jnp.where(item >= 5, v, 0.0)))

        @pl.when(is_z)
        def _():
            j = me - 20
            a = pick(jnp.where(j < 5, 5, 4), whole(step))
            on_x = (j == 1) | (j == 2) | (j == 6) | (j == 7)
            plus = (j == 1) | (j == 3) | (j == 7) | (j == 9)
            axial = (j == 0) | (j == 5)
            where = jnp.where(plus, 15, 0)
            hit = jnp.where(on_x, lane_x, lane_y) == jnp.where(axial, -1, where)
            side = jnp.where(on_x, 0, 2) + jnp.where(plus, 1, 0)
            put(step, jnp.where(hit, pick(side, a), a))

        @pl.when(me < 30)
        def _():
            for peer in far_first():
                remote(
                    ob.at[step, peer], rb.at[step, rows_of(me)], bsend.at[step], brecv.at[step], peer, layer
                ).start()
            rb[step, rows_of(me), :] = ob[step, me]

    def receive_b(step):
        @pl.when(me < 30)
        def _():
            wait_bytes(rb.at[step, pl.ds(0, 29 * 16)], brecv.at[step])

        @pl.when(me >= 30)
        def _():
            wait_bytes(rb.at[step, pl.ds(0, 30 * 16)], brecv.at[step])

    collide_all(0)
    pack_z(0)
    pack_x(0)
    pack_y(0)
    pl.semaphore_wait(barrier, (NB - 1) + 2 + 10)
    send_z(0)
    send_ten(0, 0)
    send_ten(0, 10)

    for copy in tables:
        copy.wait()
    nbf = jnp.concatenate([nbv[d] for d in range(6)] + [jnp.zeros((2, 256), jnp.int32)], axis=0).astype(f32)
    cols[...] = jnp.transpose(nbf)
    blank = jnp.zeros((48, 128), f32)
    for step in range(2):
        for first in (5, 13, 21, 29):
            rb[step, first * 16:first * 16 + 48, :] = blank

    @pl.loop(0, 256, step=32)
    def _(t):
        rows = pl.ds(pl.multiple_of(t, 32), 32)
        column = lax.broadcasted_iota(jnp.int32, (32, 256), 1).astype(f32)
        table = cols[rows, :]
        for d in range(6):
            pm[d, rows, :] = jnp.where(table[:, d:d + 1] == column, 1.0, 0.0).astype(jnp.bfloat16)

    shift_all()
    middle(0)
    receive_b(0)

    collide_faces(0)
    pack_z(1)
    send_z(1)
    pack_x(1)
    send_ten(1, 0)
    pack_y(1)
    send_ten(1, 10)

    zero = jnp.zeros((16, 128), f32)
    lane128 = lax.broadcasted_iota(jnp.int32, (1, 128), 1)

    def tile(t):
        return sens[t // 2, :, (t % 2) * 128:(t % 2) * 128 + 128] if 0 <= t < 16 else zero

    for t in range(17):
        before, here, after = tile(t - 1), tile(t), tile(t + 1)
        shifted[0, t] = jnp.where(lane128 < 32, pltpu.roll(before, 32, 1), pltpu.roll(here, 32, 1))
        shifted[1, t] = here
        shifted[2, t] = jnp.where(lane128 < 96, pltpu.roll(here, 96, 1), pltpu.roll(after, 96, 1))
        shifted[3, t] = jnp.where(lane128 < 64, pltpu.roll(here, 64, 1), pltpu.roll(after, 64, 1))

    def cut(j, pairs):
        s, t = pairs % 4, pairs // 4
        ss[j, :, :128] = shifted[s, t]
        ss[j, :, 128:] = shifted[s, t + 1]
        return pairs + oms[0, j]

    lax.fori_loop(0, NB, cut, jnp.int32(0), unroll=True)

    for half in range(2):
        rows = pl.ds(half * 8, 8)
        for peer in far_first():
            remote(ss.at[peer, rows], rs.at[me, rows], ssend, srecv, peer, layer).start()
    rs[me] = ss[me]

    shift_all()
    middle(1)

    wait_bytes(rs.at[pl.ds(0, NB - 1)], srecv)
    first = 2 * lax.fori_loop(0, NB, lambda i, acc: acc + jnp.where(i < me, oms[0, i], 0), jnp.int32(0))
    own_rows = 2 * oms[0, me]
    kf = (first + 14) // 16 - 1
    split = 16 * (kf + 1) - (first - 2)
    ka, kb = jnp.maximum(kf, 0), jnp.minimum(kf + 1, 7)

    def find(a, carry):
        ta, tb = carry
        ta = jnp.where(bxs[0, a * 8 + ka] == 0, a * 8 + ka, ta)
        tb = jnp.where(bxs[0, a * 8 + kb] == 0, a * 8 + kb, tb)
        return ta, tb

    start = lax.fori_loop(0, NB, find, (jnp.int32(0), jnp.int32(0)))
    group = lane128 // 16

    def arrange(cg, carry):
        ta, tb = carry
        parts = []
        for _ in range(8):
            parts.append(jnp.where(lane_y < split, rs[ta // 8], rs[tb // 8]))
            ta = jnp.maximum(nbx[0, ta], 0)
            tb = jnp.maximum(nbx[0, tb], 0)
        for r in range(16):
            h = r // 8
            acc = None
            for c in range(8):
                a = parts[c][:, h * 128:h * 128 + 128]
                s = ((c - r % 8) * 16) % 128
                if s:
                    a = pltpu.roll(a, s, 1)
                acc = a if acc is None else jnp.where(group == c, a, acc)
            fld[cg, r] = acc
            lanes = pl.ds(pl.multiple_of(cg * 128, 128), 128)
            hs[0, 2 * r:2 * r + 2, lanes] = acc[0:2, :]
            hs[1, 2 * r:2 * r + 2, lanes] = acc[14:16, :]
        return ta, tb

    lax.fori_loop(0, 4, arrange, start)

    to_down = remote(hs.at[0], hr.at[1], hsend.at[0], hrecv.at[1], me, down)
    to_up = remote(hs.at[1], hr.at[0], hsend.at[1], hrecv.at[0], me, up)
    to_down.start()
    to_up.start()

    lane512 = lax.broadcasted_iota(jnp.int32, (1, 512), 1)
    def along_x(v):
        m2 = jnp.where(lane512 >= 2, pltpu.roll(v, 2, 1), 0.0)
        m1 = jnp.where(lane512 >= 1, pltpu.roll(v, 1, 1), 0.0)
        p1 = jnp.where(lane512 < 511, pltpu.roll(v, 511, 1), 0.0)
        p2 = jnp.where(lane512 < 510, pltpu.roll(v, 510, 1), 0.0)
        return taps(m2, m1, v, p1, p2)

    for r in range(12):
        row = lambda q: jnp.concatenate([fld[cg, q] for cg in range(4)], axis=1)
        v = taps(row(r), row(r + 1), row(r + 2), row(r + 3), row(r + 4))
        flt[r] = jnp.where(own_rows > r, along_x(v), 0.0)

    receive_b(1)
    insert_all(1)

    to_down.wait_send()
    to_up.wait_send()
    to_up.wait_recv()
    to_down.wait_recv()
    wanted = lax.broadcasted_iota(jnp.int32, (24, 1), 0) // 2 < own_rows
    for side, there in enumerate((layer > 0, layer < NZ - 1)):
        v = hr[side]
        v = along_x(taps(v[0:24], v[2:26], v[4:28], v[6:30], v[8:32]))
        halo_out[side] = jnp.where(wanted, v, 0.0) * jnp.where(there, 1.0, 0.0)

    for step in range(2):
        wait_bytes(sa.at[step, pl.ds(0, 10 * 16)], zsend.at[step])

        @pl.when(me < 20)
        def _():
            wait_bytes(sa.at[step, pl.ds(0, 19 * 16)], asend.at[step])

        @pl.when(me >= 20)
        def _():
            wait_bytes(sa.at[step, pl.ds(0, 20 * 16)], asend.at[step])

        @pl.when(me < 30)
        def _():
            wait_bytes(ob.at[step, pl.ds(0, NB - 1)], bsend.at[step])

    wait_bytes(ss.at[pl.ds(0, NB - 1)], ssend)


def local(adjoint, velocity, porosity, block_x, neighbours, owner_map):
    f32 = jnp.float32
    vmem = pl.BlockSpec(memory_space=pltpu.VMEM)
    hbm = pl.BlockSpec(memory_space=pltpu.HBM)
    dma = pltpu.SemaphoreType.DMA
    inner, flt, halo = pl.pallas_call(
        kernel,
        out_shape=(
            jax.ShapeDtypeStruct((1, 8, 19, 16, 256), f32),
            jax.ShapeDtypeStruct((12, 16, 512), f32),
            jax.ShapeDtypeStruct((2, 24, 512), f32),
        ),
        in_specs=[hbm] * 6,
        out_specs=(vmem,) * 3,
        scratch_shapes=[
            pltpu.VMEM((8, 3, 16, 256), f32),
            pltpu.VMEM((8, 16, 256), f32),
            pltpu.VMEM((6, 1, 256), jnp.int32),
            pltpu.SMEM((1, 256), jnp.int32),
            pltpu.SMEM((1, 256), jnp.int32),
            pltpu.SMEM((1, NB), jnp.int32),
            pltpu.VMEM((256, 8), f32),
            pltpu.VMEM((8, 19, 16, 256), f32),
            pltpu.VMEM((8, 16, 256), f32),
            pltpu.VMEM((2, 42 * 16, 128), f32),
            pltpu.VMEM((2, NB, 16, 128), f32),
            pltpu.VMEM((2, NB, 16, 128), f32),
            pltpu.VMEM((2, 42 * 16, 128), f32),
            pltpu.VMEM((6, 256, 256), jnp.bfloat16),
            pltpu.VMEM((4, 17, 16, 128), f32),
            pltpu.VMEM((NB, 16, 256), f32),
            pltpu.VMEM((NB, 16, 256), f32),
            pltpu.VMEM((4, 16, 16, 128), f32),
            pltpu.VMEM((2, 32, 512), f32),
            pltpu.VMEM((2, 32, 512), f32),
            dma((3, 8)), dma((4,)),
            dma((2,)), dma((2,)), dma((2,)),
            dma((2,)), dma((2,)),
            dma, dma,
            dma((2,)), dma((2,)),
        ],
        compiler_params=pltpu.CompilerParams(
            collective_id=0, has_side_effects=True, vmem_limit_bytes=48 * 1024 * 1024
        ),
    )(*(
        pltpu.with_memory_space_constraint(array, pltpu.HBM)
        for array in (
            adjoint, velocity, porosity, jnp.transpose(neighbours, (2, 0, 1)), block_x, owner_map.reshape(1, NB)
        )
    ))
    return pl.pallas_call(
        finish,
        out_shape=(
            jax.ShapeDtypeStruct((1, 8, 19, 16, 256), f32),
            jax.ShapeDtypeStruct((1, 1, 12, 16, 512), f32),
        ),
        in_specs=[vmem] * 3,
        out_specs=(hbm, hbm),
        scratch_shapes=[
            pltpu.VMEM((12, 16, 512), f32),
            dma((9,)),
        ],
        compiler_params=pltpu.CompilerParams(vmem_limit_bytes=32 * 1024 * 1024),
    )(inner, flt, halo)


def solution(mesh):
    placed = (
        P("gz", "blk", None, None, None),
        P("gz", "blk", None, None, None),
        P("gz", "blk", None, None),
        P("gz", None),
        P("gz", None, None),
        P(),
    )
    return jax.shard_map(
        local,
        mesh=mesh,
        in_specs=placed,
        out_specs=(P("gz", "blk", None, None, None), P("gz", "blk", None, None, None)),
        check_vma=False,
    )
```
